32 devices in a mesh: expert: 8 (over z, x), dp: 4 (over y, core).
Axes of the slice: x: 2, y: 2, z: 4, core: 2. Of those that a mesh axis runs over, the one named last changes fastest.
Arguments:
- tokens: bfloat16 [1024, 7168], P('expert'), may hold values from -6 to 6
- routes: int32 [1024, 2], P('expert'), may hold values from 0 to 7, all different within a row; in each aligned block of 128 rows (0 to 127, 128 to 255, ...) at most 96 rows name the same one
- route_gates: bfloat16 [1024, 2], P('expert'), may hold values from 0.049804688 to 1
- cotangent: bfloat16 [1024, 7168], P('expert'), may hold values from -6 to 6
- weight_gate: bfloat16 [8, 7168, 1024], P('expert', None, 'dp'), may hold values from -0.0625 to 0.0625
- weight_up: bfloat16 [8, 7168, 1024], P('expert', None, 'dp'), may hold values from -0.0625 to 0.0625
- weight_down: bfloat16 [8, 1024, 7168], P('expert', 'dp'), may hold values from -0.1875 to 0.1875
Outputs:
- grad_tokens: bfloat16 [1024, 7168], P('expert', 'dp')
- grad_gate: bfloat16 [8, 7168, 1024], P('expert', None, 'dp')
- grad_up: bfloat16 [8, 7168, 1024], P('expert', None, 'dp')
- grad_down: bfloat16 [8, 1024, 7168], P('expert', 'dp')
The draws below stay inside these ranges and needn't reach their ends.
Inputs may be any that keep to these rules, and one draw needn't show every extreme that they name: `routes`: within each aligned block of 128 rows (the tokens of one index of the expert axis) every row names 2 different experts and no expert is named by more than 96 rows; in every draw some block names some expert exactly 96 times.
All inputs are finite; a program needn't handle non-finite values.
Results may differ from the reference program's by a relative error of at most 0.011.
Values may be sent and summed in bfloat16 or wider, within the bound.
A program may use at most 192 MiB of HBM per device.

```python
import math
import jax
import jax.numpy as jnp
import numpy as np
from jax import lax

D = 7168
FF = 1024
TOP_K = 2
TOK_DEV = 128
EXPERTS = 8
TOKENS = 1024
CAP = 96
FF_DEV = 256
N_EXPERT = 8
N_DP = 4


def levels(rng, extent, cuts, least, top_value):
    loudness, own = 1.0, jax.random.fold_in(rng, 6)
    for dim, blocks in cuts:
        heights = jnp.exp(jax.random.uniform(jax.random.fold_in(own, dim), (blocks,), jnp.float32, least / len(cuts), top_value / len(cuts)))
        loudness = loudness * jnp.repeat(heights, extent[dim] // blocks).reshape([-1 if axis == dim else 1 for axis in range(len(extent))])
    return loudness


def assign_block(own_key, own, number, rows, count, top, bound, lean):
    ranking = jax.random.permutation(own_key, count)
    packed, usual = shares(count, rows * top, bound, lean, True), shares(count, rows * top, bound, lean, False)
    places = jnp.arange(count)

    def named(sizes, turn):
        used = int((sizes > 0).sum())
        fixed = max(1, used // 4)
        moved = fixed + (places - fixed + turn * (used - fixed)) % max(1, count - fixed)
        return jnp.zeros((count,), jnp.int32).at[ranking[jnp.where(places < fixed, places, moved)]].set(jnp.asarray(sizes, jnp.int32))

    sizes = jnp.where(number % 4 == 0, named(packed, number // 4), named(usual, number - number // 4 - 1))
    mixed = jax.random.permutation(jax.random.fold_in(own, 3), count)
    giver, sink = mixed[0:count // 2 * 2:2], mixed[1:count // 2 * 2:2]
    slack = jnp.minimum(sizes[giver] - 1, bound - sizes[sink]) // 2
    slack = jnp.where((giver == ranking[0]) | (sink == ranking[0]) | (sizes[sink] == 0), 0, jnp.maximum(slack, 0))
    moved = jax.random.randint(jax.random.fold_in(own, 4), (count // 2,), 0, 1 << 20) % (slack + 1)
    sizes = sizes.at[giver].add(-moved).at[sink].add(moved)
    labels = jnp.searchsorted(jnp.cumsum(sizes), jnp.arange(rows * top), side="right").astype(jnp.int32)
    table = labels.reshape(top, rows).T
    table = table[jax.random.permutation(jax.random.fold_in(own, 1), rows)]
    turn = jax.random.randint(jax.random.fold_in(own, 2), (rows, 1), 0, top)
    return jnp.take_along_axis(table, (jnp.arange(top)[None, :] + turn) % top, axis=1)


def shares(number_of, total, most, skew, full):
    weights = [(1 << 20) // math.isqrt(standing ** skew) + 1 for standing in range(1, number_of + 1)]
    largest = most if full else min(most, max(-(-total // number_of), total * weights[0] // sum(weights)))
    least = 1 if total - largest >= number_of - 1 else 0
    given, spare = [largest] + [least] * (number_of - 1), total - largest - least * (number_of - 1)
    while spare > 0:
        free = [i for i in range(1, number_of) if given[i] < largest] or [i for i in range(1, number_of) if given[i] < most]
        whole, budget = sum([weights[i] for i in free]), spare
        for i in free:
            addition = min(most - given[i], max(1, budget * weights[i] // whole), spare)
            given[i] = given[i] + addition
            spare = spare - addition
    return np.array(given)


def centred(own_key, extent, deviation, most, shards=(), kind=jnp.bfloat16):
    result = jax.random.normal(own_key, extent, jnp.float32) * deviation
    if len(shards) > 0:
        result = levels(own_key, extent, shards, -0.22, 0.18) * result
    return jnp.clip(result, min=-most, max=most).astype(kind)


def setup_inputs(seed: int = 0) -> dict:
    arg_keys = jax.random.split(jax.random.key(seed), 8)
    tokens = centred(arg_keys[0], (TOKENS, D), 1.0, 6.0, ((0, 8),))
    routes_keys = jax.random.split(jax.random.fold_in(arg_keys[1], 1), TOKENS // TOK_DEV)
    routes_turns = jax.random.permutation(jax.random.fold_in(arg_keys[1], 3), TOKENS // TOK_DEV)
    routes = jax.vmap(lambda own, number: assign_block(jax.random.fold_in(arg_keys[1], 2), own, number, TOK_DEV, EXPERTS, TOP_K, CAP, 2))(routes_keys, routes_turns).reshape((TOKENS, TOP_K))
    route_gates = jnp.clip(0.049804688 + 0.9501953 * jax.random.uniform(arg_keys[2], (TOKENS, TOP_K), jnp.float32) ** levels(arg_keys[2], (TOKENS, TOP_K), ((0, 8),), -0.2, 0.2), 0.049804688, 1.0).astype(jnp.bfloat16)
    cotangent = centred(arg_keys[3], (TOKENS, D), 0.5, 6.0, ((0, 8),))
    weight_gate = centred(arg_keys[4], (EXPERTS, D, FF), D ** -0.5, 0.0625, ((0, 8), (2, 4)))
    weight_up = centred(arg_keys[5], (EXPERTS, D, FF), D ** -0.5, 0.0625, ((0, 8), (2, 4)))
    weight_down = centred(arg_keys[6], (EXPERTS, FF, D), FF ** -0.5, 0.1875, ((0, 8), (1, 4)))
    return dict(tokens=tokens, routes=routes, route_gates=route_gates, cotangent=cotangent, weight_gate=weight_gate, weight_up=weight_up, weight_down=weight_down)


def slot_table(routes):
    blocks = routes.reshape(N_EXPERT, TOK_DEV * TOP_K)
    onehot = (blocks[:, :, None] == jnp.arange(EXPERTS, dtype=jnp.int32)[None, None, :]).astype(jnp.int32)
    before = jnp.cumsum(onehot, axis=1) - onehot
    position = jnp.sum(before * onehot, axis=2).astype(jnp.int32)
    source = jnp.arange(N_EXPERT, dtype=jnp.int32)[:, None]
    receive = N_EXPERT * CAP
    slot_index = blocks * receive + source * CAP + position
    return slot_index.reshape(-1).astype(jnp.int32)


def reference(tokens, routes, route_gates, cotangent, weight_gate, weight_up, weight_down):
    receive = N_EXPERT * CAP
    total_slots = TOKENS * TOP_K
    slot_index = slot_table(routes)
    owners = jnp.full((EXPERTS * receive,), total_slots, dtype=jnp.int32).at[slot_index].set(jnp.arange(total_slots, dtype=jnp.int32))
    source_rows = (owners // TOP_K).reshape(EXPERTS, receive)
    padded_tokens = jnp.concatenate([tokens, jnp.zeros((1, D), tokens.dtype)], 0)
    padded_back = jnp.concatenate([cotangent, jnp.zeros((1, D), cotangent.dtype)], 0)
    gate_flat = jnp.concatenate([route_gates.reshape(-1), jnp.zeros((1,), route_gates.dtype)], 0)
    slot_gates = gate_flat[owners].reshape(EXPERTS, receive)

    def expert_pass(inputs):
        rows_here, gates_here, gate_matrix, up_matrix, down_matrix = inputs
        token_rows = padded_tokens[rows_here]
        back_rows = padded_back[rows_here]
        scale = gates_here.astype(jnp.float32)[:, None]
        pre_gate = jnp.dot(token_rows, gate_matrix, preferred_element_type=jnp.float32)
        pre_up = jnp.dot(token_rows, up_matrix, preferred_element_type=jnp.float32)
        sigma = jax.nn.sigmoid(pre_gate)
        activated = pre_gate * sigma
        scaled_hidden = (scale * activated * pre_up).astype(jnp.bfloat16)
        back_hidden = scale * jnp.dot(back_rows, down_matrix.T, preferred_element_type=jnp.float32)
        back_up = (back_hidden * activated).astype(jnp.bfloat16)
        back_gate = (back_hidden * pre_up * sigma * (1.0 + pre_gate * (1.0 - sigma))).astype(jnp.bfloat16)
        grad_g = jnp.dot(token_rows.T, back_gate, preferred_element_type=jnp.float32).astype(jnp.bfloat16)
        grad_u = jnp.dot(token_rows.T, back_up, preferred_element_type=jnp.float32).astype(jnp.bfloat16)
        grad_d = jnp.dot(scaled_hidden.T, back_rows, preferred_element_type=jnp.float32).astype(jnp.bfloat16)
        slot_sum = jnp.zeros((receive, D), jnp.float32)
        for group_index in range(N_DP):
            first_unit = group_index * FF_DEV
            last_unit = first_unit + FF_DEV
            partial_term = jnp.dot(back_up[:, first_unit:last_unit], up_matrix[:, first_unit:last_unit].T, preferred_element_type=jnp.float32)
            partial_term = partial_term + jnp.dot(back_gate[:, first_unit:last_unit], gate_matrix[:, first_unit:last_unit].T, preferred_element_type=jnp.float32)
            slot_sum = slot_sum + lax.optimization_barrier(partial_term.astype(jnp.bfloat16)).astype(jnp.float32)
        return grad_g, grad_u, grad_d, slot_sum.astype(jnp.bfloat16)

    grad_gate, grad_up, grad_down, slot_back = lax.map(expert_pass, (source_rows, slot_gates, weight_gate, weight_up, weight_down))
    slot_all = slot_back.reshape(EXPERTS * receive, D)
    picked = slot_all[slot_index].astype(jnp.float32).reshape(TOKENS, TOP_K, D)
    grad_tokens = jnp.sum(picked, axis=1).astype(jnp.bfloat16)
    return grad_tokens, grad_gate, grad_up, grad_down
```

```python
import jax
import jax.numpy as jnp
from jax import lax
from jax.sharding import PartitionSpec as P


def slot_layout(routes, experts, capacity):
    flat_routes = routes.reshape(-1)
    onehot = (flat_routes[:, None] == jnp.arange(experts, dtype=jnp.int32)[None, :]).astype(
        jnp.int32
    )
    before = jnp.cumsum(onehot, axis=0) - onehot
    position = jnp.sum(before * onehot, axis=1)
    slot_index = flat_routes * capacity + position
    total_slots = flat_routes.shape[0]
    owners = (
        jnp.full((experts * capacity,), total_slots, dtype=jnp.int32)
        .at[slot_index]
        .set(jnp.arange(total_slots, dtype=jnp.int32))
    )
    return (slot_index, owners)


def pad_rows(source_array, owners, top_count):
    extended = jnp.concatenate(
        [source_array, jnp.zeros((1,) + source_array.shape[1:], source_array.dtype)], 0
    )
    return extended[owners // top_count]


def per_device_slots(tokens, routes, route_gates, cotangent, weight_gate, weight_up, weight_down):
    members = lax.axis_size("expert")
    groups = lax.axis_size("dp")
    local_experts = weight_gate.shape[0]
    experts = members * local_experts
    token_rows = routes.shape[0]
    top_count = routes.shape[1]
    width = tokens.shape[1]
    quarter = width // groups
    capacity = 3 * token_rows * top_count // experts
    slot_index, owners = slot_layout(routes, experts, capacity)
    gate_flat = jnp.concatenate([route_gates.reshape(-1), jnp.zeros((1,), route_gates.dtype)], 0)
    gate_send = gate_flat[owners].reshape(experts, capacity)
    token_send = pad_rows(tokens, owners, top_count).reshape(experts, capacity, width)
    back_send = pad_rows(cotangent, owners, top_count).reshape(experts, capacity, width)
    token_arrived, back_arrived, gate_arrived = (
        lax.all_to_all(token_send, "expert", split_axis=0, concat_axis=1, tiled=True),
        lax.all_to_all(back_send, "expert", split_axis=0, concat_axis=1, tiled=True),
        lax.all_to_all(gate_send, "expert", split_axis=0, concat_axis=1, tiled=True),
    )
    scale = gate_arrived.astype(jnp.float32)[:, :, None]
    pre_gate = jnp.einsum(
        "erd,edf->erf", token_arrived, weight_gate, preferred_element_type=jnp.float32
    )
    pre_up = jnp.einsum(
        "erd,edf->erf", token_arrived, weight_up, preferred_element_type=jnp.float32
    )
    sigma = jax.nn.sigmoid(pre_gate)
    activated = pre_gate * sigma
    scaled_hidden = (scale * activated * pre_up).astype(jnp.bfloat16)
    back_hidden = scale * jnp.einsum(
        "erd,efd->erf", back_arrived, weight_down, preferred_element_type=jnp.float32
    )
    back_up = (back_hidden * activated).astype(jnp.bfloat16)
    back_gate = (back_hidden * pre_up * sigma * (1.0 + pre_gate * (1.0 - sigma))).astype(
        jnp.bfloat16
    )
    grad_gate = jnp.einsum(
        "erd,erf->edf", token_arrived, back_gate, preferred_element_type=jnp.float32
    ).astype(jnp.bfloat16)
    grad_up = jnp.einsum(
        "erd,erf->edf", token_arrived, back_up, preferred_element_type=jnp.float32
    ).astype(jnp.bfloat16)
    grad_down = jnp.einsum(
        "erf,erd->efd", scaled_hidden, back_arrived, preferred_element_type=jnp.float32
    ).astype(jnp.bfloat16)
    up_term = jnp.einsum("edf,erf->der", weight_up, back_up, preferred_element_type=jnp.float32)
    gate_term = jnp.einsum(
        "edf,erf->der", weight_gate, back_gate, preferred_element_type=jnp.float32
    )
    slot_back = lax.psum_scatter(
        (up_term + gate_term).astype(jnp.bfloat16), "dp", scatter_dimension=0, tiled=True
    )
    returned = lax.all_to_all(slot_back, "expert", split_axis=2, concat_axis=1, tiled=True)
    flat_back = returned.reshape(quarter, experts * capacity)
    picked = (
        jnp.take(flat_back, slot_index, axis=1)
        .astype(jnp.float32)
        .reshape(quarter, token_rows, top_count)
    )
    grad_tokens = jnp.sum(picked, axis=2).T.astype(jnp.bfloat16)
    return (grad_tokens, grad_gate, grad_up, grad_down)


def dot(a, b, dims):
    return lax.dot_general(a, b, (dims, ((), ())), preferred_element_type=jnp.float32)


def per_device_dense(tokens, routes, route_gates, cotangent, weight_gate, weight_up, weight_down):
    members = lax.axis_size("expert")
    groups = lax.axis_size("dp")
    me = lax.axis_index("expert")
    part = lax.axis_index("dp")
    rows, width = tokens.shape
    quarter = width // groups
    w_gate, w_up, w_down = weight_gate[0], weight_up[0], weight_down[0]

    def spread(x):
        mine = lax.dynamic_slice_in_dim(x, part * quarter, quarter, 1)
        whole = lax.all_gather(mine, ("dp", "expert"), axis=0, tiled=True)
        return whole.reshape(groups, members * rows, quarter)

    owned = (routes[:, :, None] == jnp.arange(members, dtype=routes.dtype)).astype(jnp.float32)
    weight_of = jnp.sum(owned * route_gates.astype(jnp.float32)[:, :, None], axis=1)
    weight_all = lax.all_gather(weight_of, "expert", axis=0, tiled=True)
    scale = lax.dynamic_slice_in_dim(weight_all, me, 1, 1)

    tok, cot = spread(tokens), spread(cotangent)
    blocks = [slice(i * quarter, (i + 1) * quarter) for i in range(groups)]
    pre_gate = sum(dot(tok[i], w_gate[s], ((1,), (0,))) for i, s in enumerate(blocks))
    pre_up = sum(dot(tok[i], w_up[s], ((1,), (0,))) for i, s in enumerate(blocks))
    sigma = jax.nn.sigmoid(pre_gate)
    activated = pre_gate * sigma
    scaled_hidden = (scale * activated * pre_up).astype(jnp.bfloat16)
    back_hidden = scale * sum(dot(cot[i], w_down[:, s], ((1,), (1,))) for i, s in enumerate(blocks))
    back_up = (back_hidden * activated).astype(jnp.bfloat16)
    back_gate = (back_hidden * pre_up * sigma * (1.0 + pre_gate * (1.0 - sigma))).astype(
        jnp.bfloat16
    )
    term = dot(back_up, w_up, ((1,), (1,))) + dot(back_gate, w_gate, ((1,), (1,)))
    part_sum = lax.psum_scatter(
        term.astype(jnp.bfloat16), "dp", scatter_dimension=1, tiled=True
    )
    grad_tokens = lax.psum_scatter(part_sum, "expert", scatter_dimension=0, tiled=True)
    grad_gate = jnp.concatenate(
        [dot(tok[i], back_gate, ((0,), (0,))).astype(jnp.bfloat16) for i in range(groups)], 0
    )
    grad_up = jnp.concatenate(
        [dot(tok[i], back_up, ((0,), (0,))).astype(jnp.bfloat16) for i in range(groups)], 0
    )
    grad_down = jnp.concatenate(
        [dot(scaled_hidden, cot[i], ((0,), (0,))).astype(jnp.bfloat16) for i in range(groups)], 1
    )
    return (grad_tokens, grad_gate[None], grad_up[None], grad_down[None])


def solution(mesh):
    placed = (
        P("expert", None),
        P("expert", None),
        P("expert", None),
        P("expert", None),
        P("expert", None, "dp"),
        P("expert", None, "dp"),
        P("expert", "dp", None),
    )
    return jax.shard_map(
        per_device_dense if mesh.shape["expert"] <= 8 else per_device_slots,
        mesh=mesh,
        in_specs=placed,
        out_specs=(
            P("expert", "dp"),
            P("expert", None, "dp"),
            P("expert", None, "dp"),
            P("expert", "dp", None),
        ),
        check_vma=False,
    )
```

```python
import jax
import jax.numpy as jnp
from jax import lax
from jax.experimental import pallas as pl
from jax.experimental.pallas import tpu as pltpu
from jax.sharding import PartitionSpec as P


def slot_layout(routes, experts, capacity):
    flat_routes = routes.reshape(-1)
    onehot = (flat_routes[:, None] == jnp.arange(experts, dtype=jnp.int32)[None, :]).astype(
        jnp.int32
    )
    before = jnp.cumsum(onehot, axis=0) - onehot
    position = jnp.sum(before * onehot, axis=1)
    slot_index = flat_routes * capacity + position
    total_slots = flat_routes.shape[0]
    owners = (
        jnp.full((experts * capacity,), total_slots, dtype=jnp.int32)
        .at[slot_index]
        .set(jnp.arange(total_slots, dtype=jnp.int32))
    )
    return (slot_index, owners)


def pad_rows(source_array, owners, top_count):
    extended = jnp.concatenate(
        [source_array, jnp.zeros((1,) + source_array.shape[1:], source_array.dtype)], 0
    )
    return extended[owners // top_count]


def per_device_slots(tokens, routes, route_gates, cotangent, weight_gate, weight_up, weight_down):
    members = lax.axis_size("expert")
    groups = lax.axis_size("dp")
    local_experts = weight_gate.shape[0]
    experts = members * local_experts
    token_rows = routes.shape[0]
    top_count = routes.shape[1]
    width = tokens.shape[1]
    quarter = width // groups
    capacity = 3 * token_rows * top_count // experts
    slot_index, owners = slot_layout(routes, experts, capacity)
    gate_flat = jnp.concatenate([route_gates.reshape(-1), jnp.zeros((1,), route_gates.dtype)], 0)
    gate_send = gate_flat[owners].reshape(experts, capacity)
    token_send = pad_rows(tokens, owners, top_count).reshape(experts, capacity, width)
    back_send = pad_rows(cotangent, owners, top_count).reshape(experts, capacity, width)
    token_arrived, back_arrived, gate_arrived = (
        lax.all_to_all(token_send, "expert", split_axis=0, concat_axis=1, tiled=True),
        lax.all_to_all(back_send, "expert", split_axis=0, concat_axis=1, tiled=True),
        lax.all_to_all(gate_send, "expert", split_axis=0, concat_axis=1, tiled=True),
    )
    scale = gate_arrived.astype(jnp.float32)[:, :, None]
    pre_gate = jnp.einsum(
        "erd,edf->erf", token_arrived, weight_gate, preferred_element_type=jnp.float32
    )
    pre_up = jnp.einsum(
        "erd,edf->erf", token_arrived, weight_up, preferred_element_type=jnp.float32
    )
    sigma = jax.nn.sigmoid(pre_gate)
    activated = pre_gate * sigma
    scaled_hidden = (scale * activated * pre_up).astype(jnp.bfloat16)
    back_hidden = scale * jnp.einsum(
        "erd,efd->erf", back_arrived, weight_down, preferred_element_type=jnp.float32
    )
    back_up = (back_hidden * activated).astype(jnp.bfloat16)
    back_gate = (back_hidden * pre_up * sigma * (1.0 + pre_gate * (1.0 - sigma))).astype(
        jnp.bfloat16
    )
    grad_gate = jnp.einsum(
        "erd,erf->edf", token_arrived, back_gate, preferred_element_type=jnp.float32
    ).astype(jnp.bfloat16)
    grad_up = jnp.einsum(
        "erd,erf->edf", token_arrived, back_up, preferred_element_type=jnp.float32
    ).astype(jnp.bfloat16)
    grad_down = jnp.einsum(
        "erf,erd->efd", scaled_hidden, back_arrived, preferred_element_type=jnp.float32
    ).astype(jnp.bfloat16)
    up_term = jnp.einsum("edf,erf->der", weight_up, back_up, preferred_element_type=jnp.float32)
    gate_term = jnp.einsum(
        "edf,erf->der", weight_gate, back_gate, preferred_element_type=jnp.float32
    )
    slot_back = lax.psum_scatter(
        (up_term + gate_term).astype(jnp.bfloat16), "dp", scatter_dimension=0, tiled=True
    )
    returned = lax.all_to_all(slot_back, "expert", split_axis=2, concat_axis=1, tiled=True)
    flat_back = returned.reshape(quarter, experts * capacity)
    picked = (
        jnp.take(flat_back, slot_index, axis=1)
        .astype(jnp.float32)
        .reshape(quarter, token_rows, top_count)
    )
    grad_tokens = jnp.sum(picked, axis=2).T.astype(jnp.bfloat16)
    return (grad_tokens, grad_gate, grad_up, grad_down)


def dot(a, b, dims):
    return lax.dot_general(a, b, (dims, ((), ())), preferred_element_type=jnp.float32)


MESH = pl.DeviceIdType.MESH
COLUMNS = 2
TILE = 8


def gather_events(depth):
    events = []
    for k in range(1, depth + 1):
        if k < depth:
            events += [(-k, 0), (k, 0)]
        events += [(0, 1)] if k == 1 else [(1 - k, 1), (k - 1, 1)]
    return events


def gather_kernel(depth, held, *refs):
    ins, outs = refs[:3], refs[3:6]
    got, sent, local = refs[6:]
    e, d = lax.axis_index("expert"), lax.axis_index("dp")
    z, x, y, c = e // COLUMNS, e % COLUMNS, d // 2, d % 2
    half = held // 2
    across = 3 * half // 8
    plane = half - across

    spots = {
        "up": (e + COLUMNS, d),
        "down": (e - COLUMNS, d),
        "x": (z * COLUMNS + 1 - x, d),
        "y": (e, (1 - y) * 2 + c),
        "core": (e, y * 2 + 1 - c),
    }
    have = {"up": z + 1 < depth, "down": z > 0}

    barrier = pltpu.get_barrier_semaphore()
    for name, spot in spots.items():
        def greet(spot=spot):
            pl.semaphore_signal(barrier, inc=1, device_id=spot, device_id_type=MESH)
        if name in have:
            pl.when(have[name])(greet)
        else:
            greet()
    pl.semaphore_wait(barrier, 3 + (z > 0).astype(jnp.int32) + (z + 1 < depth).astype(jnp.int32))

    def area(kind, mine):
        if kind == "plane":
            return c * half + y * across, plane
        if kind == "y":
            return c * half + (y if mine else 1 - y) * plane, across
        if kind == "core plane":
            return (c if mine else 1 - c) * half + y * across, plane
        return (c if mine else 1 - c) * half + (1 - y) * plane, across

    kinds = ("plane", "y", "core plane", "core y")
    lanes = ("up", "down", "x", "y", "core plane", "core y")

    def copy(a, lane, b, own=False, mine=True):
        kind = lane if lane in kinds else "plane"
        start, size = area(kind, mine)
        dst = outs[a].at[pl.ds(b * held + start, size)]
        src = ins[a].at[pl.ds(start, size)] if own else dst
        return pltpu.make_async_remote_copy(
            src_ref=src,
            dst_ref=dst,
            send_sem=sent.at[a, lanes.index(lane), b],
            recv_sem=got.at[a, kinds.index(kind), b],
            device_id=spots["core" if lane[:4] == "core" else lane],
            device_id_type=MESH,
        )

    def arrived(a, kind, b):
        lane = "x" if kind == "plane" else kind
        copy(a, lane, b, mine=False).wait_recv()

    def maybe(cond, fn):
        pl.when(cond)(fn)

    for a in range(3):
        maybe(have["up"], lambda a=a: copy(a, "up", e, True).start())
        maybe(have["down"], lambda a=a: copy(a, "down", e, True).start())
        copy(a, "x", e, True).start()
    keep = [
        pltpu.make_async_copy(ins[a], outs[a].at[pl.ds(e * held, held)], local.at[a])
        for a in range(3)
    ]
    for k in keep:
        k.start()

    events = gather_events(depth)

    def where(event):
        off, other = event
        zz = z + off
        block = zz * COLUMNS + (1 - x if other else x)
        return (zz >= 0) & (zz < depth), block

    def onward(event):
        off, other = event
        if other or off == 0:
            return None
        return "up" if off < 0 else "down"

    def plane_event(event):
        ok, b = where(event)
        lane = onward(event)

        @pl.when(ok)
        def _():
            for a in range(3):
                arrived(a, "plane", b)
                if lane:
                    maybe(have[lane], lambda a=a: copy(a, lane, b).start())
                    copy(a, "x", b).start()
                copy(a, "y", b).start()
                copy(a, "core plane", b).start()

    def y_event(event):
        ok, b = where(event)

        @pl.when(ok)
        def _():
            for a in range(3):
                arrived(a, "y", b)
                copy(a, "core y", b).start()

    lag = 3
    for i, event in enumerate(events):
        plane_event(event)
        if i >= lag:
            y_event(events[i - lag])
    for event in events[len(events) - lag:]:
        y_event(event)

    for k in keep:
        k.wait()
    for a in range(3):
        maybe(have["up"], lambda a=a: copy(a, "up", e, True).wait_send())
        maybe(have["down"], lambda a=a: copy(a, "down", e, True).wait_send())
        copy(a, "x", e, True).wait_send()
    for event in events:
        ok, b = where(event)
        lane = onward(event)

        @pl.when(ok)
        def _(b=b, lane=lane):
            for a in range(3):
                arrived(a, "core plane", b)
                arrived(a, "core y", b)
                if lane:
                    maybe(have[lane], lambda a=a: copy(a, lane, b).wait_send())
                    copy(a, "x", b).wait_send()
                copy(a, "y", b).wait_send()
                copy(a, "core plane", b).wait_send()
                copy(a, "core y", b).wait_send()


def gather_all(arrays):
    members = lax.axis_size("expert")
    held = arrays[0].shape[0] // TILE
    tiled = [v.reshape(held, TILE, v.shape[1]) for v in arrays]
    outs = pl.pallas_call(
        lambda *refs: gather_kernel(members // COLUMNS, held, *refs),
        out_shape=[
            jax.ShapeDtypeStruct((members * held, TILE, v.shape[1]), v.dtype) for v in arrays
        ],
        in_specs=[pl.BlockSpec(memory_space=pl.ANY)] * 3,
        out_specs=[pl.BlockSpec(memory_space=pl.ANY)] * 3,
        scratch_shapes=[
            pltpu.SemaphoreType.DMA((3, 4, members)),
            pltpu.SemaphoreType.DMA((3, 6, members)),
            pltpu.SemaphoreType.DMA((3,)),
        ],
        compiler_params=pltpu.CompilerParams(collective_id=0, has_side_effects=True),
        name="gather_all",
    )(*tiled)
    return [v.reshape(v.shape[0] * TILE, v.shape[2]) for v in outs]


def per_device_dense(tokens, routes, route_gates, cotangent, weight_gate, weight_up, weight_down):
    me = lax.axis_index("expert")
    w_gate, w_up, w_down = weight_gate[0], weight_up[0], weight_down[0]

    owned = (routes[:, :, None] == jnp.arange(128, dtype=routes.dtype)).astype(jnp.float32)
    weight_of = jnp.sum(owned * route_gates.astype(jnp.float32)[:, :, None], axis=1)
    tok, cot, weight_all = gather_all([tokens, cotangent, weight_of.astype(jnp.bfloat16)])
    scale = lax.dynamic_slice_in_dim(weight_all, me, 1, 1).astype(jnp.float32)
    pre_gate = dot(tok, w_gate, ((1,), (0,)))
    pre_up = dot(tok, w_up, ((1,), (0,)))
    sigma = jax.nn.sigmoid(pre_gate)
    activated = pre_gate * sigma
    scaled_hidden = (scale * activated * pre_up).astype(jnp.bfloat16)
    back_hidden = scale * dot(cot, w_down, ((1,), (1,)))
    back_up = (back_hidden * activated).astype(jnp.bfloat16)
    back_gate = (back_hidden * pre_up * sigma * (1.0 + pre_gate * (1.0 - sigma))).astype(
        jnp.bfloat16
    )
    term = dot(back_up, w_up, ((1,), (1,))) + dot(back_gate, w_gate, ((1,), (1,)))
    part_sum = lax.psum_scatter(
        term.astype(jnp.bfloat16), "dp", scatter_dimension=1, tiled=True
    )
    grad_tokens = lax.psum_scatter(part_sum, "expert", scatter_dimension=0, tiled=True)
    grad_gate = dot(tok, back_gate, ((0,), (0,))).astype(jnp.bfloat16)
    grad_up = dot(tok, back_up, ((0,), (0,))).astype(jnp.bfloat16)
    grad_down = dot(scaled_hidden, cot, ((0,), (0,))).astype(jnp.bfloat16)
    return (grad_tokens, grad_gate[None], grad_up[None], grad_down[None])


def solution(mesh):
    placed = (
        P("expert", None),
        P("expert", None),
        P("expert", None),
        P("expert", None),
        P("expert", None, "dp"),
        P("expert", None, "dp"),
        P("expert", "dp", None),
    )
    return jax.shard_map(
        per_device_dense if mesh.shape["expert"] <= 8 else per_device_slots,
        mesh=mesh,
        in_specs=placed,
        out_specs=(
            P("expert", "dp"),
            P("expert", None, "dp"),
            P("expert", None, "dp"),
            P("expert", "dp", None),
        ),
        check_vma=False,
    )
```

```python
import jax
import jax.numpy as jnp
from jax import lax
from jax.experimental import pallas as pl
from jax.experimental.pallas import tpu as pltpu
from jax.sharding import PartitionSpec as P


def slot_layout(routes, experts, capacity):
    flat_routes = routes.reshape(-1)
    onehot = (flat_routes[:, None] == jnp.arange(experts, dtype=jnp.int32)[None, :]).astype(
        jnp.int32
    )
    before = jnp.cumsum(onehot, axis=0) - onehot
    position = jnp.sum(before * onehot, axis=1)
    slot_index = flat_routes * capacity + position
    total_slots = flat_routes.shape[0]
    owners = (
        jnp.full((experts * capacity,), total_slots, dtype=jnp.int32)
        .at[slot_index]
        .set(jnp.arange(total_slots, dtype=jnp.int32))
    )
    return (slot_index, owners)


def pad_rows(source_array, owners, top_count):
    extended = jnp.concatenate(
        [source_array, jnp.zeros((1,) + source_array.shape[1:], source_array.dtype)], 0
    )
    return extended[owners // top_count]


def per_device_slots(tokens, routes, route_gates, cotangent, weight_gate, weight_up, weight_down):
    members = lax.axis_size("expert")
    groups = lax.axis_size("dp")
    local_experts = weight_gate.shape[0]
    experts = members * local_experts
    token_rows = routes.shape[0]
    top_count = routes.shape[1]
    width = tokens.shape[1]
    quarter = width // groups
    capacity = 3 * token_rows * top_count // experts
    slot_index, owners = slot_layout(routes, experts, capacity)
    gate_flat = jnp.concatenate([route_gates.reshape(-1), jnp.zeros((1,), route_gates.dtype)], 0)
    gate_send = gate_flat[owners].reshape(experts, capacity)
    token_send = pad_rows(tokens, owners, top_count).reshape(experts, capacity, width)
    back_send = pad_rows(cotangent, owners, top_count).reshape(experts, capacity, width)
    token_arrived, back_arrived, gate_arrived = (
        lax.all_to_all(token_send, "expert", split_axis=0, concat_axis=1, tiled=True),
        lax.all_to_all(back_send, "expert", split_axis=0, concat_axis=1, tiled=True),
        lax.all_to_all(gate_send, "expert", split_axis=0, concat_axis=1, tiled=True),
    )
    scale = gate_arrived.astype(jnp.float32)[:, :, None]
    pre_gate = jnp.einsum(
        "erd,edf->erf", token_arrived, weight_gate, preferred_element_type=jnp.float32
    )
    pre_up = jnp.einsum(
        "erd,edf->erf", token_arrived, weight_up, preferred_element_type=jnp.float32
    )
    sigma = jax.nn.sigmoid(pre_gate)
    activated = pre_gate * sigma
    scaled_hidden = (scale * activated * pre_up).astype(jnp.bfloat16)
    back_hidden = scale * jnp.einsum(
        "erd,efd->erf", back_arrived, weight_down, preferred_element_type=jnp.float32
    )
    back_up = (back_hidden * activated).astype(jnp.bfloat16)
    back_gate = (back_hidden * pre_up * sigma * (1.0 + pre_gate * (1.0 - sigma))).astype(
        jnp.bfloat16
    )
    grad_gate = jnp.einsum(
        "erd,erf->edf", token_arrived, back_gate, preferred_element_type=jnp.float32
    ).astype(jnp.bfloat16)
    grad_up = jnp.einsum(
        "erd,erf->edf", token_arrived, back_up, preferred_element_type=jnp.float32
    ).astype(jnp.bfloat16)
    grad_down = jnp.einsum(
        "erf,erd->efd", scaled_hidden, back_arrived, preferred_element_type=jnp.float32
    ).astype(jnp.bfloat16)
    up_term = jnp.einsum("edf,erf->der", weight_up, back_up, preferred_element_type=jnp.float32)
    gate_term = jnp.einsum(
        "edf,erf->der", weight_gate, back_gate, preferred_element_type=jnp.float32
    )
    slot_back = lax.psum_scatter(
        (up_term + gate_term).astype(jnp.bfloat16), "dp", scatter_dimension=0, tiled=True
    )
    returned = lax.all_to_all(slot_back, "expert", split_axis=2, concat_axis=1, tiled=True)
    flat_back = returned.reshape(quarter, experts * capacity)
    picked = (
        jnp.take(flat_back, slot_index, axis=1)
        .astype(jnp.float32)
        .reshape(quarter, token_rows, top_count)
    )
    grad_tokens = jnp.sum(picked, axis=2).T.astype(jnp.bfloat16)
    return (grad_tokens, grad_gate, grad_up, grad_down)


def dot(a, b, dims):
    return lax.dot_general(a, b, (dims, ((), ())), preferred_element_type=jnp.float32)


MESH = pl.DeviceIdType.MESH
COLUMNS = 2
TILE = 8


def gather_events(depth):
    events = []
    for k in range(1, depth + 1):
        if k < depth:
            events += [(-k, 0), (k, 0)]
        events += [(0, 1)] if k == 1 else [(1 - k, 1), (k - 1, 1)]
    return events


def gather_kernel(depth, held, *refs):
    ins, outs = refs[:3], refs[3:6]
    got, sent, local = refs[6:]
    e, d = lax.axis_index("expert"), lax.axis_index("dp")
    z, x, y, c = e // COLUMNS, e % COLUMNS, d // 2, d % 2
    half = held // 2
    across = 3 * half // 8
    plane = half - across

    spots = {
        "up": (e + COLUMNS, d),
        "down": (e - COLUMNS, d),
        "x": (z * COLUMNS + 1 - x, d),
        "y": (e, (1 - y) * 2 + c),
        "core": (e, y * 2 + 1 - c),
    }
    have = {"up": z + 1 < depth, "down": z > 0}

    barrier = pltpu.get_barrier_semaphore()
    for name, spot in spots.items():
        def greet(spot=spot):
            pl.semaphore_signal(barrier, inc=1, device_id=spot, device_id_type=MESH)
        if name in have:
            pl.when(have[name])(greet)
        else:
            greet()
    pl.semaphore_wait(barrier, 3 + (z > 0).astype(jnp.int32) + (z + 1 < depth).astype(jnp.int32))

    def area(kind, mine):
        if kind == "plane":
            return c * half + y * across, plane
        if kind == "y":
            return c * half + (y if mine else 1 - y) * plane, across
        if kind == "core plane":
            return (c if mine else 1 - c) * half + y * across, plane
        return (c if mine else 1 - c) * half + (1 - y) * plane, across

    kinds = ("plane", "y", "core plane", "core y")
    lanes = ("up", "down", "x", "y", "core plane", "core y")

    def copy(a, lane, b, own=False, mine=True):
        kind = lane if lane in kinds else "plane"
        start, size = area(kind, mine)
        dst = outs[a].at[pl.ds(b * held + start, size)]
        src = ins[a].at[pl.ds(start, size)] if own else dst
        return pltpu.make_async_remote_copy(
            src_ref=src,
            dst_ref=dst,
            send_sem=sent.at[a, lanes.index(lane), b],
            recv_sem=got.at[a, kinds.index(kind), b],
            device_id=spots["core" if lane[:4] == "core" else lane],
            device_id_type=MESH,
        )

    def arrived(a, kind, b):
        lane = "x" if kind == "plane" else kind
        copy(a, lane, b, mine=False).wait_recv()

    def maybe(cond, fn):
        pl.when(cond)(fn)

    for a in range(3):
        maybe(have["up"], lambda a=a: copy(a, "up", e, True).start())
        maybe(have["down"], lambda a=a: copy(a, "down", e, True).start())
        copy(a, "x", e, True).start()
    keep = [
        pltpu.make_async_copy(ins[a], outs[a].at[pl.ds(e * held, held)], local.at[a])
        for a in range(3)
    ]
    for k in keep:
        k.start()

    events = gather_events(depth)

    def where(event):
        off, other = event
        zz = z + off
        block = zz * COLUMNS + (1 - x if other else x)
        return (zz >= 0) & (zz < depth), block

    def onward(event):
        off, other = event
        if other or off == 0:
            return None
        return "up" if off < 0 else "down"

    def plane_event(event):
        ok, b = where(event)
        lane = onward(event)

        @pl.when(ok)
        def _():
            for a in range(3):
                arrived(a, "plane", b)
                if lane:
                    maybe(have[lane], lambda a=a: copy(a, lane, b).start())
                    copy(a, "x", b).start()
                copy(a, "y", b).start()
                copy(a, "core plane", b).start()

    def y_event(event):
        ok, b = where(event)

        @pl.when(ok)
        def _():
            for a in range(3):
                arrived(a, "y", b)
                copy(a, "core y", b).start()

    lag = 3
    for i, event in enumerate(events):
        plane_event(event)
        if i >= lag:
            y_event(events[i - lag])
    for event in events[len(events) - lag:]:
        y_event(event)

    for k in keep:
        k.wait()
    for a in range(3):
        maybe(have["up"], lambda a=a: copy(a, "up", e, True).wait_send())
        maybe(have["down"], lambda a=a: copy(a, "down", e, True).wait_send())
        copy(a, "x", e, True).wait_send()
    for event in events:
        ok, b = where(event)
        lane = onward(event)

        @pl.when(ok)
        def _(b=b, lane=lane):
            for a in range(3):
                arrived(a, "core plane", b)
                arrived(a, "core y", b)
                if lane:
                    maybe(have[lane], lambda a=a: copy(a, lane, b).wait_send())
                    copy(a, "x", b).wait_send()
                copy(a, "y", b).wait_send()
                copy(a, "core plane", b).wait_send()
                copy(a, "core y", b).wait_send()


def gather_all(arrays):
    members = lax.axis_size("expert")
    held = arrays[0].shape[0] // TILE
    tiled = [v.reshape(held, TILE, v.shape[1]) for v in arrays]
    outs = pl.pallas_call(
        lambda *refs: gather_kernel(members // COLUMNS, held, *refs),
        out_shape=[
            jax.ShapeDtypeStruct((members * held, TILE, v.shape[1]), v.dtype) for v in arrays
        ],
        in_specs=[pl.BlockSpec(memory_space=pl.ANY)] * 3,
        out_specs=[pl.BlockSpec(memory_space=pl.ANY)] * 3,
        scratch_shapes=[
            pltpu.SemaphoreType.DMA((3, 4, members)),
            pltpu.SemaphoreType.DMA((3, 6, members)),
            pltpu.SemaphoreType.DMA((3,)),
        ],
        compiler_params=pltpu.CompilerParams(collective_id=0, has_side_effects=True),
        name="gather_all",
    )(*tiled)
    return [v.reshape(v.shape[0] * TILE, v.shape[2]) for v in outs]


def add_into(ref, other):
    step = 16

    def body(i, carry):
        rows = pl.ds(pl.multiple_of(i * step, step), step)
        total = ref[rows, :].astype(jnp.float32) + other[rows, :].astype(jnp.float32)
        ref[rows, :] = total.astype(ref.dtype)
        return carry

    lax.fori_loop(0, ref.shape[0] // step, body, 0)


def scatter_kernel(
    depth, back_up, back_gate, w_up, w_gate, out, part, from_core, y_one, x_one, x_two, y_two,
    from_below, from_above, sent, got,
):
    e, d = lax.axis_index("expert"), lax.axis_index("dp")
    z, x, y, c = e // COLUMNS, e % COLUMNS, d // 2, d % 2
    half, quarter = part.shape[-2:]
    spots = {
        "up": (e + COLUMNS, d),
        "down": (e - COLUMNS, d),
        "x": (z * COLUMNS + 1 - x, d),
        "y": (e, (1 - y) * 2 + c),
        "core": (e, y * 2 + 1 - c),
    }
    have = {"up": z + 1 < depth, "down": z > 0}
    barrier = pltpu.get_barrier_semaphore()
    for name, spot in spots.items():
        def greet(spot=spot):
            pl.semaphore_signal(barrier, inc=1, device_id=spot, device_id_type=MESH)
        if name in have:
            pl.when(have[name])(greet)
        else:
            greet()
    pl.semaphore_wait(barrier, 3 + (z > 0).astype(jnp.int32) + (z + 1 < depth).astype(jnp.int32))

    def copy(q, n, src, dst, lane):
        return pltpu.make_async_remote_copy(
            src_ref=src, dst_ref=dst, send_sem=sent.at[q, n], recv_sem=got.at[q, n],
            device_id=spots[lane], device_id_type=MESH,
        )

    def core_copy(q, yy):
        return copy(q, yy, part.at[q, yy, 1 - c], from_core.at[q, yy], "core")

    def y_one_copy(q):
        return copy(q, 2, part.at[q, 1 - y, c, 0], y_one.at[q], "y")

    def x_two_copy(q, yy):
        return copy(q, 3 + yy, part.at[q, yy, c, 1, 1 - x], x_two.at[q, yy], "x")

    def x_one_copy(q):
        return copy(q, 5, part.at[q, y, c, 0, 1 - x], x_one.at[q], "x")

    def y_two_copy(q):
        return copy(q, 6, part.at[q, 1 - y, c, 1, x], y_two.at[q], "y")

    def up_copy(q, t):
        return copy(q, 7 + t, part.at[q, y, c, t, x], from_below.at[q, t], "up")

    def down_copy(q, t):
        return copy(q, 9 + t, part.at[q, y, c, t, x], from_above.at[q, t], "down")

    tile = 256
    rows = 4 * half

    def terms(q, yy, cc):
        def body(n, carry):
            first = pl.multiple_of((yy * 2 + cc) * quarter + n * tile, tile)
            nt = (((1,), (1,)), ((), ()))
            taken = pl.ds(q * rows, rows)
            term = lax.dot_general(
                back_up[taken, :], w_up[pl.ds(first, tile), :], nt,
                preferred_element_type=jnp.float32,
            ) + lax.dot_general(
                back_gate[taken, :], w_gate[pl.ds(first, tile), :], nt,
                preferred_element_type=jnp.float32,
            )
            term = term.astype(part.dtype)
            columns = pl.ds(pl.multiple_of(n * tile, tile), tile)
            for xx in range(2):
                for t in range(2):
                    at = (xx * 2 + t) * half
                    part[q, yy, cc, t, xx, :, columns] = term[at : at + half]
            return carry

        lax.fori_loop(0, quarter // tile, body, 0)

    def stage_a(q):
        for yy in range(2):
            terms(q, yy, 1 - c)
            core_copy(q, yy).start()
        for yy in range(2):
            terms(q, yy, c)

    def stage_b(q):
        for yy in range(2):
            core_copy(q, yy).wait_recv()
            for t in range(2):
                for xx in range(2):
                    add_into(part.at[q, yy, c, t, xx], from_core.at[q, yy, t, xx])
        y_one_copy(q).start()
        for yy in range(2):
            x_two_copy(q, yy).start()

    def stage_c(q):
        y_one_copy(q).wait_recv()
        for xx in range(2):
            add_into(part.at[q, y, c, 0, xx], y_one.at[q, xx])
        x_one_copy(q).start()
        for yy in range(2):
            x_two_copy(q, yy).wait_recv()
            add_into(part.at[q, yy, c, 1, x], x_two.at[q, yy])
        y_two_copy(q).start()

    def stage_d(q):
        x_one_copy(q).wait_recv()
        add_into(part.at[q, y, c, 0, x], x_one.at[q])
        y_two_copy(q).wait_recv()
        add_into(part.at[q, y, c, 1, x], y_two.at[q])

    def below(q):
        for t in range(2):
            up_copy(q, t).wait_recv()
            add_into(part.at[q, y, c, t, x], from_below.at[q, t])

    def above(q):
        for t in range(2):
            down_copy(q, t).wait_recv()
            add_into(part.at[q, y, c, t, x], from_above.at[q, t])

    def stage_e(q):
        @pl.when(z < q)
        def _():
            pl.when(z > 0)(lambda: below(q))
            for t in range(2):
                up_copy(q, t).start()

        @pl.when(z > q)
        def _():
            pl.when(z + 1 < depth)(lambda: above(q))
            for t in range(2):
                down_copy(q, t).start()

    order = []
    low, high = 0, depth - 1
    while low <= high:
        order += [low] if low == high else [low, high]
        low, high = low + 1, high - 1
    stages = (stage_a, stage_b, stage_c, stage_d, stage_e)
    for beat in range(depth + len(stages) - 1):
        for s, stage in enumerate(stages):
            if 0 <= beat - s < depth:
                stage(order[beat - s])

    for q in range(depth):
        @pl.when(z == q)
        def _(q=q):
            pl.when(z > 0)(lambda: below(q))
            pl.when(z + 1 < depth)(lambda: above(q))
            for t in range(2):
                out[pl.ds(t * half, half), :] = part[q, y, c, t, x]

    for q in range(depth):
        for yy in range(2):
            core_copy(q, yy).wait_send()
            x_two_copy(q, yy).wait_send()
        y_one_copy(q).wait_send()
        x_one_copy(q).wait_send()
        y_two_copy(q).wait_send()
        for t in range(2):
            pl.when(z < q)(lambda q=q, t=t: up_copy(q, t).wait_send())
            pl.when(z > q)(lambda q=q, t=t: down_copy(q, t).wait_send())


def scatter_sum(back_up, back_gate, w_up, w_gate):
    members = lax.axis_size("expert")
    depth = members // COLUMNS
    rows = back_up.shape[0] // members
    width = w_up.shape[0]
    quarter, half = width // 4, rows // 2
    kind = back_up.dtype
    whole = pl.BlockSpec(memory_space=pltpu.VMEM)
    return pl.pallas_call(
        lambda *refs: scatter_kernel(depth, *refs),
        out_shape=jax.ShapeDtypeStruct((rows, quarter), kind),
        in_specs=[whole] * 4,
        out_specs=whole,
        scratch_shapes=[
            pltpu.VMEM((depth, 2, 2, 2, 2, half, quarter), kind),
            pltpu.VMEM((depth, 2, 2, 2, half, quarter), kind),
            pltpu.VMEM((depth, 2, half, quarter), kind),
            pltpu.VMEM((depth, half, quarter), kind),
            pltpu.VMEM((depth, 2, half, quarter), kind),
            pltpu.VMEM((depth, half, quarter), kind),
            pltpu.VMEM((depth, 2, half, quarter), kind),
            pltpu.VMEM((depth, 2, half, quarter), kind),
            pltpu.SemaphoreType.DMA((depth, 11)),
            pltpu.SemaphoreType.DMA((depth, 11)),
        ],
        compiler_params=pltpu.CompilerParams(
            collective_id=1, has_side_effects=True, vmem_limit_bytes=56 * 2**20
        ),
        name="scatter_sum",
    )(back_up, back_gate, w_up, w_gate)


def per_device_dense(tokens, routes, route_gates, cotangent, weight_gate, weight_up, weight_down):
    me = lax.axis_index("expert")
    w_gate, w_up, w_down = weight_gate[0], weight_up[0], weight_down[0]

    owned = (routes[:, :, None] == jnp.arange(128, dtype=routes.dtype)).astype(jnp.float32)
    weight_of = jnp.sum(owned * route_gates.astype(jnp.float32)[:, :, None], axis=1)
    tok, cot, weight_all = gather_all([tokens, cotangent, weight_of.astype(jnp.bfloat16)])
    scale = lax.dynamic_slice_in_dim(weight_all, me, 1, 1).astype(jnp.float32)
    pre_gate = dot(tok, w_gate, ((1,), (0,)))
    pre_up = dot(tok, w_up, ((1,), (0,)))
    sigma = jax.nn.sigmoid(pre_gate)
    activated = pre_gate * sigma
    scaled_hidden = (scale * activated * pre_up).astype(jnp.bfloat16)
    back_hidden = scale * dot(cot, w_down, ((1,), (1,)))
    back_up = (back_hidden * activated).astype(jnp.bfloat16)
    back_gate = (back_hidden * pre_up * sigma * (1.0 + pre_gate * (1.0 - sigma))).astype(
        jnp.bfloat16
    )
    grad_tokens = scatter_sum(back_up, back_gate, w_up, w_gate)
    grad_gate = dot(tok, back_gate, ((0,), (0,))).astype(jnp.bfloat16)
    grad_up = dot(tok, back_up, ((0,), (0,))).astype(jnp.bfloat16)
    grad_down = dot(scaled_hidden, cot, ((0,), (0,))).astype(jnp.bfloat16)
    return (grad_tokens, grad_gate[None], grad_up[None], grad_down[None])


def solution(mesh):
    placed = (
        P("expert", None),
        P("expert", None),
        P("expert", None),
        P("expert", None),
        P("expert", None, "dp"),
        P("expert", None, "dp"),
        P("expert", "dp", None),
    )
    return jax.shard_map(
        per_device_dense if mesh.shape["expert"] <= 8 else per_device_slots,
        mesh=mesh,
        in_specs=placed,
        out_specs=(
            P("expert", "dp"),
            P("expert", None, "dp"),
            P("expert", None, "dp"),
            P("expert", "dp", None),
        ),
        check_vma=False,
    )
```

```python
import jax
import jax.numpy as jnp
from jax import lax
from jax.experimental import pallas as pl
from jax.experimental.pallas import tpu as pltpu
from jax.sharding import PartitionSpec as P


def slot_layout(routes, experts, capacity):
    flat_routes = routes.reshape(-1)
    onehot = (flat_routes[:, None] == jnp.arange(experts, dtype=jnp.int32)[None, :]).astype(
        jnp.int32
    )
    before = jnp.cumsum(onehot, axis=0) - onehot
    position = jnp.sum(before * onehot, axis=1)
    slot_index = flat_routes * capacity + position
    total_slots = flat_routes.shape[0]
    owners = (
        jnp.full((experts * capacity,), total_slots, dtype=jnp.int32)
        .at[slot_index]
        .set(jnp.arange(total_slots, dtype=jnp.int32))
    )
    return (slot_index, owners)


def pad_rows(source_array, owners, top_count):
    extended = jnp.concatenate(
        [source_array, jnp.zeros((1,) + source_array.shape[1:], source_array.dtype)], 0
    )
    return extended[owners // top_count]


def per_device_slots(tokens, routes, route_gates, cotangent, weight_gate, weight_up, weight_down):
    members = lax.axis_size("expert")
    groups = lax.axis_size("dp")
    local_experts = weight_gate.shape[0]
    experts = members * local_experts
    token_rows = routes.shape[0]
    top_count = routes.shape[1]
    width = tokens.shape[1]
    quarter = width // groups
    capacity = 3 * token_rows * top_count // experts
    slot_index, owners = slot_layout(routes, experts, capacity)
    gate_flat = jnp.concatenate([route_gates.reshape(-1), jnp.zeros((1,), route_gates.dtype)], 0)
    gate_send = gate_flat[owners].reshape(experts, capacity)
    token_send = pad_rows(tokens, owners, top_count).reshape(experts, capacity, width)
    back_send = pad_rows(cotangent, owners, top_count).reshape(experts, capacity, width)
    token_arrived, back_arrived, gate_arrived = (
        lax.all_to_all(token_send, "expert", split_axis=0, concat_axis=1, tiled=True),
        lax.all_to_all(back_send, "expert", split_axis=0, concat_axis=1, tiled=True),
        lax.all_to_all(gate_send, "expert", split_axis=0, concat_axis=1, tiled=True),
    )
    scale = gate_arrived.astype(jnp.float32)[:, :, None]
    pre_gate = jnp.einsum(
        "erd,edf->erf", token_arrived, weight_gate, preferred_element_type=jnp.float32
    )
    pre_up = jnp.einsum(
        "erd,edf->erf", token_arrived, weight_up, preferred_element_type=jnp.float32
    )
    sigma = jax.nn.sigmoid(pre_gate)
    activated = pre_gate * sigma
    scaled_hidden = (scale * activated * pre_up).astype(jnp.bfloat16)
    back_hidden = scale * jnp.einsum(
        "erd,efd->erf", back_arrived, weight_down, preferred_element_type=jnp.float32
    )
    back_up = (back_hidden * activated).astype(jnp.bfloat16)
    back_gate = (back_hidden * pre_up * sigma * (1.0 + pre_gate * (1.0 - sigma))).astype(
        jnp.bfloat16
    )
    grad_gate = jnp.einsum(
        "erd,erf->edf", token_arrived, back_gate, preferred_element_type=jnp.float32
    ).astype(jnp.bfloat16)
    grad_up = jnp.einsum(
        "erd,erf->edf", token_arrived, back_up, preferred_element_type=jnp.float32
    ).astype(jnp.bfloat16)
    grad_down = jnp.einsum(
        "erf,erd->efd", scaled_hidden, back_arrived, preferred_element_type=jnp.float32
    ).astype(jnp.bfloat16)
    up_term = jnp.einsum("edf,erf->der", weight_up, back_up, preferred_element_type=jnp.float32)
    gate_term = jnp.einsum(
        "edf,erf->der", weight_gate, back_gate, preferred_element_type=jnp.float32
    )
    slot_back = lax.psum_scatter(
        (up_term + gate_term).astype(jnp.bfloat16), "dp", scatter_dimension=0, tiled=True
    )
    returned = lax.all_to_all(slot_back, "expert", split_axis=2, concat_axis=1, tiled=True)
    flat_back = returned.reshape(quarter, experts * capacity)
    picked = (
        jnp.take(flat_back, slot_index, axis=1)
        .astype(jnp.float32)
        .reshape(quarter, token_rows, top_count)
    )
    grad_tokens = jnp.sum(picked, axis=2).T.astype(jnp.bfloat16)
    return (grad_tokens, grad_gate, grad_up, grad_down)


def dot(a, b, dims):
    return lax.dot_general(a, b, (dims, ((), ())), preferred_element_type=jnp.float32)


MESH = pl.DeviceIdType.MESH
COLUMNS = 2
TILE = 8


def gather_events(depth):
    events = []
    for k in range(1, depth + 1):
        if k < depth:
            events += [(-k, 0), (k, 0)]
        events += [(0, 1)] if k == 1 else [(1 - k, 1), (k - 1, 1)]
    return events


def gather_kernel(depth, held, *refs):
    ins, outs = refs[:3], refs[3:6]
    got, sent, local = refs[6:]
    e, d = lax.axis_index("expert"), lax.axis_index("dp")
    z, x, y, c = e // COLUMNS, e % COLUMNS, d // 2, d % 2
    half = held // 2
    across = 3 * half // 8
    plane = half - across

    spots = {
        "up": (e + COLUMNS, d),
        "down": (e - COLUMNS, d),
        "x": (z * COLUMNS + 1 - x, d),
        "y": (e, (1 - y) * 2 + c),
        "core": (e, y * 2 + 1 - c),
    }
    have = {"up": z + 1 < depth, "down": z > 0}

    barrier = pltpu.get_barrier_semaphore()
    for name, spot in spots.items():
        def greet(spot=spot):
            pl.semaphore_signal(barrier, inc=1, device_id=spot, device_id_type=MESH)
        if name in have:
            pl.when(have[name])(greet)
        else:
            greet()
    pl.semaphore_wait(barrier, 3 + (z > 0).astype(jnp.int32) + (z + 1 < depth).astype(jnp.int32))

    def area(kind, mine):
        if kind == "plane":
            return c * half + y * across, plane
        if kind == "y":
            return c * half + (y if mine else 1 - y) * plane, across
        if kind == "core plane":
            return (c if mine else 1 - c) * half + y * across, plane
        return (c if mine else 1 - c) * half + (1 - y) * plane, across

    kinds = ("plane", "y", "core plane", "core y")
    lanes = ("up", "down", "x", "y", "core plane", "core y")

    def copy(a, lane, b, own=False, mine=True):
        kind = lane if lane in kinds else "plane"
        start, size = area(kind, mine)
        dst = outs[a].at[pl.ds(b * held + start, size)]
        src = ins[a].at[pl.ds(start, size)] if own else dst
        return pltpu.make_async_remote_copy(
            src_ref=src,
            dst_ref=dst,
            send_sem=sent.at[a, lanes.index(lane), b],
            recv_sem=got.at[a, kinds.index(kind), b],
            device_id=spots["core" if lane[:4] == "core" else lane],
            device_id_type=MESH,
        )

    def arrived(a, kind, b):
        lane = "x" if kind == "plane" else kind
        copy(a, lane, b, mine=False).wait_recv()

    def maybe(cond, fn):
        pl.when(cond)(fn)

    for a in range(3):
        maybe(have["up"], lambda a=a: copy(a, "up", e, True).start())
        maybe(have["down"], lambda a=a: copy(a, "down", e, True).start())
        copy(a, "x", e, True).start()
    keep = [
        pltpu.make_async_copy(ins[a], outs[a].at[pl.ds(e * held, held)], local.at[a])
        for a in range(3)
    ]
    for k in keep:
        k.start()

    events = gather_events(depth)

    def where(event):
        off, other = event
        zz = z + off
        block = zz * COLUMNS + (1 - x if other else x)
        return (zz >= 0) & (zz < depth), block

    def onward(event):
        off, other = event
        if other or off == 0:
            return None
        return "up" if off < 0 else "down"

    def plane_event(event):
        ok, b = where(event)
        lane = onward(event)

        @pl.when(ok)
        def _():
            for a in range(3):
                arrived(a, "plane", b)
                if lane:
                    maybe(have[lane], lambda a=a: copy(a, lane, b).start())
                    copy(a, "x", b).start()
                copy(a, "y", b).start()
                copy(a, "core plane", b).start()

    def y_event(event):
        ok, b = where(event)

        @pl.when(ok)
        def _():
            for a in range(3):
                arrived(a, "y", b)
                copy(a, "core y", b).start()

    lag = 3
    for i, event in enumerate(events):
        plane_event(event)
        if i >= lag:
            y_event(events[i - lag])
    for event in events[len(events) - lag:]:
        y_event(event)

    for k in keep:
        k.wait()
    for a in range(3):
        maybe(have["up"], lambda a=a: copy(a, "up", e, True).wait_send())
        maybe(have["down"], lambda a=a: copy(a, "down", e, True).wait_send())
        copy(a, "x", e, True).wait_send()
    for event in events:
        ok, b = where(event)
        lane = onward(event)

        @pl.when(ok)
        def _(b=b, lane=lane):
            for a in range(3):
                arrived(a, "core plane", b)
                arrived(a, "core y", b)
                if lane:
                    maybe(have[lane], lambda a=a: copy(a, lane, b).wait_send())
                    copy(a, "x", b).wait_send()
                copy(a, "y", b).wait_send()
                copy(a, "core plane", b).wait_send()
                copy(a, "core y", b).wait_send()


def gather_all(arrays):
    members = lax.axis_size("expert")
    held = arrays[0].shape[0] // TILE
    tiled = [v.reshape(held, TILE, v.shape[1]) for v in arrays]
    outs = pl.pallas_call(
        lambda *refs: gather_kernel(members // COLUMNS, held, *refs),
        out_shape=[
            jax.ShapeDtypeStruct((members * held, TILE, v.shape[1]), v.dtype) for v in arrays
        ],
        in_specs=[pl.BlockSpec(memory_space=pl.ANY)] * 3,
        out_specs=[pl.BlockSpec(memory_space=pl.ANY)] * 3,
        scratch_shapes=[
            pltpu.SemaphoreType.DMA((3, 4, members)),
            pltpu.SemaphoreType.DMA((3, 6, members)),
            pltpu.SemaphoreType.DMA((3,)),
        ],
        compiler_params=pltpu.CompilerParams(collective_id=0, has_side_effects=True),
        name="gather_all",
    )(*tiled)
    return [v.reshape(v.shape[0] * TILE, v.shape[2]) for v in outs]


def add_into(ref, other):
    step = 16

    def body(i, carry):
        rows = pl.ds(pl.multiple_of(i * step, step), step)
        total = ref[rows, :].astype(jnp.float32) + other[rows, :].astype(jnp.float32)
        ref[rows, :] = total.astype(ref.dtype)
        return carry

    lax.fori_loop(0, ref.shape[0] // step, body, 0)


def scatter_kernel(
    depth, back_up, back_gate, w_up, w_gate, out, part, from_core, y_one, x_one, x_two, y_two,
    from_below, from_above, sent, got,
):
    e, d = lax.axis_index("expert"), lax.axis_index("dp")
    z, x, y, c = e // COLUMNS, e % COLUMNS, d // 2, d % 2
    half, quarter = part.shape[-2:]
    spots = {
        "up": (e + COLUMNS, d),
        "down": (e - COLUMNS, d),
        "x": (z * COLUMNS + 1 - x, d),
        "y": (e, (1 - y) * 2 + c),
        "core": (e, y * 2 + 1 - c),
    }
    have = {"up": z + 1 < depth, "down": z > 0}
    barrier = pltpu.get_barrier_semaphore()
    for name, spot in spots.items():
        def greet(spot=spot):
            pl.semaphore_signal(barrier, inc=1, device_id=spot, device_id_type=MESH)
        if name in have:
            pl.when(have[name])(greet)
        else:
            greet()
    pl.semaphore_wait(barrier, 3 + (z > 0).astype(jnp.int32) + (z + 1 < depth).astype(jnp.int32))

    def copy(q, n, src, dst, lane):
        return pltpu.make_async_remote_copy(
            src_ref=src, dst_ref=dst, send_sem=sent.at[q, n], recv_sem=got.at[q, n],
            device_id=spots[lane], device_id_type=MESH,
        )

    def core_copy(q, yy):
        return copy(q, yy, part.at[q, yy, 1 - c], from_core.at[q, yy], "core")

    def y_one_copy(q):
        return copy(q, 2, part.at[q, 1 - y, c, 0], y_one.at[q], "y")

    def x_two_copy(q, yy):
        return copy(q, 3 + yy, part.at[q, yy, c, 1, 1 - x], x_two.at[q, yy], "x")

    def x_one_copy(q):
        return copy(q, 5, part.at[q, y, c, 0, 1 - x], x_one.at[q], "x")

    def y_two_copy(q):
        return copy(q, 6, part.at[q, 1 - y, c, 1, x], y_two.at[q], "y")

    def up_copy(q, t):
        return copy(q, 7 + t, part.at[q, y, c, t, x], from_below.at[q, t], "up")

    def down_copy(q, t):
        return copy(q, 9 + t, part.at[q, y, c, t, x], from_above.at[q, t], "down")

    tile = 256
    rows = 4 * half

    def terms(q, yy, cc):
        def body(n, carry):
            first = pl.multiple_of((yy * 2 + cc) * quarter + n * tile, tile)
            nt = (((1,), (1,)), ((), ()))
            taken = pl.ds(q * rows, rows)
            term = lax.dot_general(
                back_up[taken, :], w_up[pl.ds(first, tile), :], nt,
                preferred_element_type=jnp.float32,
            ) + lax.dot_general(
                back_gate[taken, :], w_gate[pl.ds(first, tile), :], nt,
                preferred_element_type=jnp.float32,
            )
            term = term.astype(part.dtype)
            columns = pl.ds(pl.multiple_of(n * tile, tile), tile)
            for xx in range(2):
                for t in range(2):
                    at = (xx * 2 + t) * half
                    part[q, yy, cc, t, xx, :, columns] = term[at : at + half]
            return carry

        lax.fori_loop(0, quarter // tile, body, 0)

    def stage_a(q):
        for yy in range(2):
            terms(q, yy, 1 - c)
            core_copy(q, yy).start()
        for yy in range(2):
            terms(q, yy, c)

    def stage_b(q):
        for yy in range(2):
            core_copy(q, yy).wait_recv()
            for t in range(2):
                for xx in range(2):
                    add_into(part.at[q, yy, c, t, xx], from_core.at[q, yy, t, xx])
        y_one_copy(q).start()
        for yy in range(2):
            x_two_copy(q, yy).start()

    def stage_c(q):
        y_one_copy(q).wait_recv()
        for xx in range(2):
            add_into(part.at[q, y, c, 0, xx], y_one.at[q, xx])
        x_one_copy(q).start()
        for yy in range(2):
            x_two_copy(q, yy).wait_recv()
            add_into(part.at[q, yy, c, 1, x], x_two.at[q, yy])
        y_two_copy(q).start()

    def stage_d(q):
        x_one_copy(q).wait_recv()
        add_into(part.at[q, y, c, 0, x], x_one.at[q])
        y_two_copy(q).wait_recv()
        add_into(part.at[q, y, c, 1, x], y_two.at[q])

    def below(q):
        for t in range(2):
            up_copy(q, t).wait_recv()
            add_into(part.at[q, y, c, t, x], from_below.at[q, t])

    def above(q):
        for t in range(2):
            down_copy(q, t).wait_recv()
            add_into(part.at[q, y, c, t, x], from_above.at[q, t])

    def stage_e(q):
        @pl.when(z < q)
        def _():
            pl.when(z > 0)(lambda: below(q))
            for t in range(2):
                up_copy(q, t).start()

        @pl.when(z > q)
        def _():
            pl.when(z + 1 < depth)(lambda: above(q))
            for t in range(2):
                down_copy(q, t).start()

    order = []
    low, high = 0, depth - 1
    while low <= high:
        order += [low] if low == high else [low, high]
        low, high = low + 1, high - 1
    stages = (stage_a, stage_b, stage_c, stage_d, stage_e)
    for beat in range(depth + len(stages) - 1):
        for s, stage in enumerate(stages):
            if 0 <= beat - s < depth:
                stage(order[beat - s])

    for q in range(depth):
        @pl.when(z == q)
        def _(q=q):
            pl.when(z > 0)(lambda: below(q))
            pl.when(z + 1 < depth)(lambda: above(q))
            for t in range(2):
                out[pl.ds(t * half, half), :] = part[q, y, c, t, x]

    for q in range(depth):
        for yy in range(2):
            core_copy(q, yy).wait_send()
            x_two_copy(q, yy).wait_send()
        y_one_copy(q).wait_send()
        x_one_copy(q).wait_send()
        y_two_copy(q).wait_send()
        for t in range(2):
            pl.when(z < q)(lambda q=q, t=t: up_copy(q, t).wait_send())
            pl.when(z > q)(lambda q=q, t=t: down_copy(q, t).wait_send())


def scatter_sum(back_up, back_gate, w_up, w_gate):
    members = lax.axis_size("expert")
    depth = members // COLUMNS
    rows = back_up.shape[0] // members
    width = w_up.shape[0]
    quarter, half = width // 4, rows // 2
    kind = back_up.dtype
    whole = pl.BlockSpec(memory_space=pltpu.VMEM)
    return pl.pallas_call(
        lambda *refs: scatter_kernel(depth, *refs),
        out_shape=jax.ShapeDtypeStruct((rows, quarter), kind),
        in_specs=[whole] * 4,
        out_specs=whole,
        scratch_shapes=[
            pltpu.VMEM((depth, 2, 2, 2, 2, half, quarter), kind),
            pltpu.VMEM((depth, 2, 2, 2, half, quarter), kind),
            pltpu.VMEM((depth, 2, half, quarter), kind),
            pltpu.VMEM((depth, half, quarter), kind),
            pltpu.VMEM((depth, 2, half, quarter), kind),
            pltpu.VMEM((depth, half, quarter), kind),
            pltpu.VMEM((depth, 2, half, quarter), kind),
            pltpu.VMEM((depth, 2, half, quarter), kind),
            pltpu.SemaphoreType.DMA((depth, 11)),
            pltpu.SemaphoreType.DMA((depth, 11)),
        ],
        compiler_params=pltpu.CompilerParams(
            collective_id=1, has_side_effects=True, vmem_limit_bytes=56 * 2**20
        ),
        name="scatter_sum",
    )(back_up, back_gate, w_up, w_gate)


def hidden_kernel(
    tok, cot, w_gate, w_up, w_down, scale, back_up, back_gate, back_t, hidden_t, gate, up, back
):
    step = pl.program_id(0)

    @pl.when(step == 0)
    def _():
        gate[...] = jnp.zeros_like(gate)
        up[...] = jnp.zeros_like(up)
        back[...] = jnp.zeros_like(back)

    gate[...] += dot(tok[...], w_gate[...], ((1,), (0,)))
    up[...] += dot(tok[...], w_up[...], ((1,), (0,)))
    back[...] += dot(cot[...], w_down[...], ((1,), (1,)))

    @pl.when(step == pl.num_programs(0) - 1)
    def _():
        size, units = 128, gate.shape[1]

        def body(i, carry):
            rows = pl.ds(pl.multiple_of(i * size, size), size)
            pre_gate, pre_up, factor = gate[rows, :], up[rows, :], scale[rows, :]
            sigma = jax.nn.sigmoid(pre_gate)
            activated = pre_gate * sigma
            back_hidden = factor * back[rows, :]
            hidden = (factor * activated * pre_up).astype(jnp.bfloat16)
            down_up = (back_hidden * activated).astype(jnp.bfloat16)
            down_gate = (
                back_hidden * pre_up * sigma * (1.0 + pre_gate * (1.0 - sigma))
            ).astype(jnp.bfloat16)
            back_up[rows, :] = down_up
            back_gate[rows, :] = down_gate
            hidden_t[:, rows] = hidden.T
            back_t[:units, rows] = down_gate.T
            back_t[units:, rows] = down_up.T
            return carry

        lax.fori_loop(0, gate.shape[0] // size, body, 0)


def hidden_grads(tok, cot, w_gate, w_up, w_down, scale):
    rows, width = tok.shape
    units = w_gate.shape[1]
    tile = 512
    kind = tok.dtype
    across = pl.BlockSpec((rows, tile), lambda i: (0, i))
    along = pl.BlockSpec((tile, units), lambda i: (i, 0))

    def fixed(shape):
        return pl.BlockSpec(shape, lambda i: (0, 0))

    shapes = [(rows, units), (rows, units), (2 * units, rows), (units, rows)]
    return pl.pallas_call(
        hidden_kernel,
        grid=(width // tile,),
        out_shape=[jax.ShapeDtypeStruct(s, kind) for s in shapes],
        in_specs=[
            across, across, along, along, pl.BlockSpec((units, tile), lambda i: (0, i)),
            fixed((rows, 1)),
        ],
        out_specs=[fixed(s) for s in shapes],
        scratch_shapes=[pltpu.VMEM((rows, units), jnp.float32)] * 3,
        compiler_params=pltpu.CompilerParams(vmem_limit_bytes=40 * 2**20),
        name="hidden_grads",
    )(tok, cot, w_gate, w_up, w_down, scale)


def weight_kernel(tok, cot, back_t, hidden_t, grad_gate, grad_up, grad_down):
    units = hidden_t.shape[0]
    both = dot(back_t[...], tok[...], ((1,), (0,))).astype(grad_gate.dtype)
    grad_gate[...] = both[:units].T
    grad_up[...] = both[units:].T
    grad_down[...] = dot(hidden_t[...], cot[...], ((1,), (0,))).astype(grad_down.dtype)


def weight_grads(tok, cot, back_t, hidden_t):
    rows, width = tok.shape
    units = hidden_t.shape[0]
    tile = 512
    kind = tok.dtype
    across = pl.BlockSpec((rows, tile), lambda i: (0, i))
    along = pl.BlockSpec((tile, units), lambda i: (i, 0))
    return pl.pallas_call(
        weight_kernel,
        grid=(width // tile,),
        out_shape=[
            jax.ShapeDtypeStruct((width, units), kind),
            jax.ShapeDtypeStruct((width, units), kind),
            jax.ShapeDtypeStruct((units, width), kind),
        ],
        in_specs=[
            across, across,
            pl.BlockSpec((2 * units, rows), lambda i: (0, 0)),
            pl.BlockSpec((units, rows), lambda i: (0, 0)),
        ],
        out_specs=[along, along, pl.BlockSpec((units, tile), lambda i: (0, i))],
        compiler_params=pltpu.CompilerParams(vmem_limit_bytes=40 * 2**20),
        name="weight_grads",
    )(tok, cot, back_t, hidden_t)


def per_device_dense(tokens, routes, route_gates, cotangent, weight_gate, weight_up, weight_down):
    me = lax.axis_index("expert")
    w_gate, w_up, w_down = weight_gate[0], weight_up[0], weight_down[0]

    owned = (routes[:, :, None] == jnp.arange(128, dtype=routes.dtype)).astype(jnp.float32)
    weight_of = jnp.sum(owned * route_gates.astype(jnp.float32)[:, :, None], axis=1)
    tok, cot, weight_all = gather_all([tokens, cotangent, weight_of.astype(jnp.bfloat16)])
    scale = lax.dynamic_slice_in_dim(weight_all, me, 1, 1).astype(jnp.float32)
    back_up, back_gate, back_t, hidden_t = hidden_grads(tok, cot, w_gate, w_up, w_down, scale)
    grad_tokens = scatter_sum(back_up, back_gate, w_up, w_gate)
    grad_gate, grad_up, grad_down = weight_grads(tok, cot, back_t, hidden_t)
    return (grad_tokens, grad_gate[None], grad_up[None], grad_down[None])


def solution(mesh):
    placed = (
        P("expert", None),
        P("expert", None),
        P("expert", None),
        P("expert", None),
        P("expert", None, "dp"),
        P("expert", None, "dp"),
        P("expert", "dp", None),
    )
    return jax.shard_map(
        per_device_dense if mesh.shape["expert"] <= 8 else per_device_slots,
        mesh=mesh,
        in_specs=placed,
        out_specs=(
            P("expert", "dp"),
            P("expert", None, "dp"),
            P("expert", None, "dp"),
            P("expert", "dp", None),
        ),
        check_vma=False,
    )
```

```python
import jax
import jax.numpy as jnp
from jax import lax
from jax.experimental import pallas as pl
from jax.experimental.pallas import tpu as pltpu
from jax.sharding import PartitionSpec as P


def slot_layout(routes, experts, capacity):
    flat_routes = routes.reshape(-1)
    onehot = (flat_routes[:, None] == jnp.arange(experts, dtype=jnp.int32)[None, :]).astype(
        jnp.int32
    )
    before = jnp.cumsum(onehot, axis=0) - onehot
    position = jnp.sum(before * onehot, axis=1)
    slot_index = flat_routes * capacity + position
    total_slots = flat_routes.shape[0]
    owners = (
        jnp.full((experts * capacity,), total_slots, dtype=jnp.int32)
        .at[slot_index]
        .set(jnp.arange(total_slots, dtype=jnp.int32))
    )
    return (slot_index, owners)


def pad_rows(source_array, owners, top_count):
    extended = jnp.concatenate(
        [source_array, jnp.zeros((1,) + source_array.shape[1:], source_array.dtype)], 0
    )
    return extended[owners // top_count]


def per_device_slots(tokens, routes, route_gates, cotangent, weight_gate, weight_up, weight_down):
    members = lax.axis_size("expert")
    groups = lax.axis_size("dp")
    local_experts = weight_gate.shape[0]
    experts = members * local_experts
    token_rows = routes.shape[0]
    top_count = routes.shape[1]
    width = tokens.shape[1]
    quarter = width // groups
    capacity = 3 * token_rows * top_count // experts
    slot_index, owners = slot_layout(routes, experts, capacity)
    gate_flat = jnp.concatenate([route_gates.reshape(-1), jnp.zeros((1,), route_gates.dtype)], 0)
    gate_send = gate_flat[owners].reshape(experts, capacity)
    token_send = pad_rows(tokens, owners, top_count).reshape(experts, capacity, width)
    back_send = pad_rows(cotangent, owners, top_count).reshape(experts, capacity, width)
    token_arrived, back_arrived, gate_arrived = (
        lax.all_to_all(token_send, "expert", split_axis=0, concat_axis=1, tiled=True),
        lax.all_to_all(back_send, "expert", split_axis=0, concat_axis=1, tiled=True),
        lax.all_to_all(gate_send, "expert", split_axis=0, concat_axis=1, tiled=True),
    )
    scale = gate_arrived.astype(jnp.float32)[:, :, None]
    pre_gate = jnp.einsum(
        "erd,edf->erf", token_arrived, weight_gate, preferred_element_type=jnp.float32
    )
    pre_up = jnp.einsum(
        "erd,edf->erf", token_arrived, weight_up, preferred_element_type=jnp.float32
    )
    sigma = jax.nn.sigmoid(pre_gate)
    activated = pre_gate * sigma
    scaled_hidden = (scale * activated * pre_up).astype(jnp.bfloat16)
    back_hidden = scale * jnp.einsum(
        "erd,efd->erf", back_arrived, weight_down, preferred_element_type=jnp.float32
    )
    back_up = (back_hidden * activated).astype(jnp.bfloat16)
    back_gate = (back_hidden * pre_up * sigma * (1.0 + pre_gate * (1.0 - sigma))).astype(
        jnp.bfloat16
    )
    grad_gate = jnp.einsum(
        "erd,erf->edf", token_arrived, back_gate, preferred_element_type=jnp.float32
    ).astype(jnp.bfloat16)
    grad_up = jnp.einsum(
        "erd,erf->edf", token_arrived, back_up, preferred_element_type=jnp.float32
    ).astype(jnp.bfloat16)
    grad_down = jnp.einsum(
        "erf,erd->efd", scaled_hidden, back_arrived, preferred_element_type=jnp.float32
    ).astype(jnp.bfloat16)
    up_term = jnp.einsum("edf,erf->der", weight_up, back_up, preferred_element_type=jnp.float32)
    gate_term = jnp.einsum(
        "edf,erf->der", weight_gate, back_gate, preferred_element_type=jnp.float32
    )
    slot_back = lax.psum_scatter(
        (up_term + gate_term).astype(jnp.bfloat16), "dp", scatter_dimension=0, tiled=True
    )
    returned = lax.all_to_all(slot_back, "expert", split_axis=2, concat_axis=1, tiled=True)
    flat_back = returned.reshape(quarter, experts * capacity)
    picked = (
        jnp.take(flat_back, slot_index, axis=1)
        .astype(jnp.float32)
        .reshape(quarter, token_rows, top_count)
    )
    grad_tokens = jnp.sum(picked, axis=2).T.astype(jnp.bfloat16)
    return (grad_tokens, grad_gate, grad_up, grad_down)


def dot(a, b, dims):
    return lax.dot_general(a, b, (dims, ((), ())), preferred_element_type=jnp.float32)


MESH = pl.DeviceIdType.MESH
COLUMNS = 2
TILE = 8


def gather_events(depth):
    events = []
    for k in range(1, depth + 1):
        if k < depth:
            events += [(-k, 0), (k, 0)]
        events += [(0, 1)] if k == 1 else [(1 - k, 1), (k - 1, 1)]
    return events


def gather_kernel(depth, held, *refs):
    ins, outs = refs[:3], refs[3:6]
    got, sent, local = refs[6:]
    e, d = lax.axis_index("expert"), lax.axis_index("dp")
    z, x, y, c = e // COLUMNS, e % COLUMNS, d // 2, d % 2
    half = held // 2
    across = 3 * half // 8
    plane = half - across

    spots = {
        "up": (e + COLUMNS, d),
        "down": (e - COLUMNS, d),
        "x": (z * COLUMNS + 1 - x, d),
        "y": (e, (1 - y) * 2 + c),
        "core": (e, y * 2 + 1 - c),
    }
    have = {"up": z + 1 < depth, "down": z > 0}

    barrier = pltpu.get_barrier_semaphore()
    for name, spot in spots.items():
        def greet(spot=spot):
            pl.semaphore_signal(barrier, inc=1, device_id=spot, device_id_type=MESH)
        if name in have:
            pl.when(have[name])(greet)
        else:
            greet()
    pl.semaphore_wait(barrier, 3 + (z > 0).astype(jnp.int32) + (z + 1 < depth).astype(jnp.int32))

    def area(kind, mine):
        if kind == "plane":
            return c * half + y * across, plane
        if kind == "y":
            return c * half + (y if mine else 1 - y) * plane, across
        if kind == "core plane":
            return (c if mine else 1 - c) * half + y * across, plane
        return (c if mine else 1 - c) * half + (1 - y) * plane, across

    kinds = ("plane", "y", "core plane", "core y")
    lanes = ("up", "down", "x", "y", "core plane", "core y")

    def copy(a, lane, b, own=False, mine=True):
        kind = lane if lane in kinds else "plane"
        start, size = area(kind, mine)
        dst = outs[a].at[pl.ds(b * held + start, size)]
        src = ins[a].at[pl.ds(start, size)] if own else dst
        return pltpu.make_async_remote_copy(
            src_ref=src,
            dst_ref=dst,
            send_sem=sent.at[a, lanes.index(lane), b],
            recv_sem=got.at[a, kinds.index(kind), b],
            device_id=spots["core" if lane[:4] == "core" else lane],
            device_id_type=MESH,
        )

    def arrived(a, kind, b):
        lane = "x" if kind == "plane" else kind
        copy(a, lane, b, mine=False).wait_recv()

    def maybe(cond, fn):
        pl.when(cond)(fn)

    for a in range(3):
        maybe(have["up"], lambda a=a: copy(a, "up", e, True).start())
        maybe(have["down"], lambda a=a: copy(a, "down", e, True).start())
        copy(a, "x", e, True).start()
    keep = [
        pltpu.make_async_copy(ins[a], outs[a].at[pl.ds(e * held, held)], local.at[a])
        for a in range(3)
    ]
    for k in keep:
        k.start()

    events = gather_events(depth)

    def where(event):
        off, other = event
        zz = z + off
        block = zz * COLUMNS + (1 - x if other else x)
        return (zz >= 0) & (zz < depth), block

    def onward(event):
        off, other = event
        if other or off == 0:
            return None
        return "up" if off < 0 else "down"

    def plane_event(event):
        ok, b = where(event)
        lane = onward(event)

        @pl.when(ok)
        def _():
            for a in range(3):
                arrived(a, "plane", b)
                if lane:
                    maybe(have[lane], lambda a=a: copy(a, lane, b).start())
                    copy(a, "x", b).start()
                copy(a, "y", b).start()
                copy(a, "core plane", b).start()

    def y_event(event):
        ok, b = where(event)

        @pl.when(ok)
        def _():
            for a in range(3):
                arrived(a, "y", b)
                copy(a, "core y", b).start()

    for event in events:
        plane_event(event)
    for event in events:
        y_event(event)

    for k in keep:
        k.wait()
    for a in range(3):
        maybe(have["up"], lambda a=a: copy(a, "up", e, True).wait_send())
        maybe(have["down"], lambda a=a: copy(a, "down", e, True).wait_send())
        copy(a, "x", e, True).wait_send()
    for event in events:
        ok, b = where(event)
        lane = onward(event)

        @pl.when(ok)
        def _(b=b, lane=lane):
            for a in range(3):
                arrived(a, "core plane", b)
                arrived(a, "core y", b)
                if lane:
                    maybe(have[lane], lambda a=a: copy(a, lane, b).wait_send())
                    copy(a, "x", b).wait_send()
                copy(a, "y", b).wait_send()
                copy(a, "core plane", b).wait_send()
                copy(a, "core y", b).wait_send()


def gather_all(arrays):
    members = lax.axis_size("expert")
    held = arrays[0].shape[0] // TILE
    tiled = [v.reshape(held, TILE, v.shape[1]) for v in arrays]
    outs = pl.pallas_call(
        lambda *refs: gather_kernel(members // COLUMNS, held, *refs),
        out_shape=[
            jax.ShapeDtypeStruct((members * held, TILE, v.shape[1]), v.dtype) for v in arrays
        ],
        in_specs=[pl.BlockSpec(memory_space=pl.ANY)] * 3,
        out_specs=[pl.BlockSpec(memory_space=pl.ANY)] * 3,
        scratch_shapes=[
            pltpu.SemaphoreType.DMA((3, 4, members)),
            pltpu.SemaphoreType.DMA((3, 6, members)),
            pltpu.SemaphoreType.DMA((3,)),
        ],
        compiler_params=pltpu.CompilerParams(collective_id=0, has_side_effects=True),
        name="gather_all",
    )(*tiled)
    return [v.reshape(v.shape[0] * TILE, v.shape[2]) for v in outs]


def add_into(ref, other):
    step = 16

    def body(i, carry):
        rows = pl.ds(pl.multiple_of(i * step, step), step)
        total = ref[rows, :].astype(jnp.float32) + other[rows, :].astype(jnp.float32)
        ref[rows, :] = total.astype(ref.dtype)
        return carry

    lax.fori_loop(0, ref.shape[0] // step, body, 0)


def scatter_kernel(
    depth, back_up, back_gate, w_up, w_gate, out, part, from_core, y_one, x_one, x_two, y_two,
    from_below, from_above, sent, got,
):
    e, d = lax.axis_index("expert"), lax.axis_index("dp")
    z, x, y, c = e // COLUMNS, e % COLUMNS, d // 2, d % 2
    half, quarter = part.shape[-2:]
    spots = {
        "up": (e + COLUMNS, d),
        "down": (e - COLUMNS, d),
        "x": (z * COLUMNS + 1 - x, d),
        "y": (e, (1 - y) * 2 + c),
        "core": (e, y * 2 + 1 - c),
    }
    have = {"up": z + 1 < depth, "down": z > 0}
    barrier = pltpu.get_barrier_semaphore()
    for name, spot in spots.items():
        def greet(spot=spot):
            pl.semaphore_signal(barrier, inc=1, device_id=spot, device_id_type=MESH)
        if name in have:
            pl.when(have[name])(greet)
        else:
            greet()
    pl.semaphore_wait(barrier, 3 + (z > 0).astype(jnp.int32) + (z + 1 < depth).astype(jnp.int32))

    def copy(q, n, src, dst, lane):
        return pltpu.make_async_remote_copy(
            src_ref=src, dst_ref=dst, send_sem=sent.at[q, n], recv_sem=got.at[q, n],
            device_id=spots[lane], device_id_type=MESH,
        )

    def core_copy(q, yy):
        return copy(q, yy, part.at[q, yy, 1 - c], from_core.at[q, yy], "core")

    def y_one_copy(q):
        return copy(q, 2, part.at[q, 1 - y, c, 0], y_one.at[q], "y")

    def x_two_copy(q, yy):
        return copy(q, 3 + yy, part.at[q, yy, c, 1, 1 - x], x_two.at[q, yy], "x")

    def x_one_copy(q):
        return copy(q, 5, part.at[q, y, c, 0, 1 - x], x_one.at[q], "x")

    def y_two_copy(q):
        return copy(q, 6, part.at[q, 1 - y, c, 1, x], y_two.at[q], "y")

    def up_copy(q, t):
        return copy(q, 7 + t, part.at[q, y, c, t, x], from_below.at[q, t], "up")

    def down_copy(q, t):
        return copy(q, 9 + t, part.at[q, y, c, t, x], from_above.at[q, t], "down")

    tile = 256
    rows = 4 * half

    def terms(q, yy, cc):
        def body(n, carry):
            first = pl.multiple_of((yy * 2 + cc) * quarter + n * tile, tile)
            nt = (((1,), (1,)), ((), ()))
            taken = pl.ds(q * rows, rows)
            term = lax.dot_general(
                back_up[taken, :], w_up[pl.ds(first, tile), :], nt,
                preferred_element_type=jnp.float32,
            ) + lax.dot_general(
                back_gate[taken, :], w_gate[pl.ds(first, tile), :], nt,
                preferred_element_type=jnp.float32,
            )
            term = term.astype(part.dtype)
            columns = pl.ds(pl.multiple_of(n * tile, tile), tile)
            for xx in range(2):
                for t in range(2):
                    at = (xx * 2 + t) * half
                    part[q, yy, cc, t, xx, :, columns] = term[at : at + half]
            return carry

        lax.fori_loop(0, quarter // tile, body, 0)

    def stage_a(q):
        for yy in range(2):
            terms(q, yy, 1 - c)
            core_copy(q, yy).start()
        for yy in range(2):
            terms(q, yy, c)

    def stage_b(q):
        for yy in range(2):
            core_copy(q, yy).wait_recv()
            for t in range(2):
                for xx in range(2):
                    add_into(part.at[q, yy, c, t, xx], from_core.at[q, yy, t, xx])
        y_one_copy(q).start()
        for yy in range(2):
            x_two_copy(q, yy).start()

    def stage_c(q):
        y_one_copy(q).wait_recv()
        for xx in range(2):
            add_into(part.at[q, y, c, 0, xx], y_one.at[q, xx])
        x_one_copy(q).start()
        for yy in range(2):
            x_two_copy(q, yy).wait_recv()
            add_into(part.at[q, yy, c, 1, x], x_two.at[q, yy])
        y_two_copy(q).start()

    def stage_d(q):
        x_one_copy(q).wait_recv()
        add_into(part.at[q, y, c, 0, x], x_one.at[q])
        y_two_copy(q).wait_recv()
        add_into(part.at[q, y, c, 1, x], y_two.at[q])

    def below(q):
        for t in range(2):
            up_copy(q, t).wait_recv()
            add_into(part.at[q, y, c, t, x], from_below.at[q, t])

    def above(q):
        for t in range(2):
            down_copy(q, t).wait_recv()
            add_into(part.at[q, y, c, t, x], from_above.at[q, t])

    def stage_e(q):
        @pl.when(z < q)
        def _():
            pl.when(z > 0)(lambda: below(q))
            for t in range(2):
                up_copy(q, t).start()

        @pl.when(z > q)
        def _():
            pl.when(z + 1 < depth)(lambda: above(q))
            for t in range(2):
                down_copy(q, t).start()

    order = []
    low, high = 0, depth - 1
    while low <= high:
        order += [low] if low == high else [low, high]
        low, high = low + 1, high - 1
    stages = (stage_a, stage_b, stage_c, stage_d, stage_e)
    for beat in range(depth + len(stages) - 1):
        for s, stage in enumerate(stages):
            if 0 <= beat - s < depth:
                stage(order[beat - s])

    for q in range(depth):
        @pl.when(z == q)
        def _(q=q):
            pl.when(z > 0)(lambda: below(q))
            pl.when(z + 1 < depth)(lambda: above(q))
            for t in range(2):
                out[pl.ds(t * half, half), :] = part[q, y, c, t, x]

    for q in range(depth):
        for yy in range(2):
            core_copy(q, yy).wait_send()
            x_two_copy(q, yy).wait_send()
        y_one_copy(q).wait_send()
        x_one_copy(q).wait_send()
        y_two_copy(q).wait_send()
        for t in range(2):
            pl.when(z < q)(lambda q=q, t=t: up_copy(q, t).wait_send())
            pl.when(z > q)(lambda q=q, t=t: down_copy(q, t).wait_send())


def scatter_sum(back_up, back_gate, w_up, w_gate):
    members = lax.axis_size("expert")
    depth = members // COLUMNS
    rows = back_up.shape[0] // members
    width = w_up.shape[0]
    quarter, half = width // 4, rows // 2
    kind = back_up.dtype
    whole = pl.BlockSpec(memory_space=pltpu.VMEM)
    return pl.pallas_call(
        lambda *refs: scatter_kernel(depth, *refs),
        out_shape=jax.ShapeDtypeStruct((rows, quarter), kind),
        in_specs=[whole] * 4,
        out_specs=whole,
        scratch_shapes=[
            pltpu.VMEM((depth, 2, 2, 2, 2, half, quarter), kind),
            pltpu.VMEM((depth, 2, 2, 2, half, quarter), kind),
            pltpu.VMEM((depth, 2, half, quarter), kind),
            pltpu.VMEM((depth, half, quarter), kind),
            pltpu.VMEM((depth, 2, half, quarter), kind),
            pltpu.VMEM((depth, half, quarter), kind),
            pltpu.VMEM((depth, 2, half, quarter), kind),
            pltpu.VMEM((depth, 2, half, quarter), kind),
            pltpu.SemaphoreType.DMA((depth, 11)),
            pltpu.SemaphoreType.DMA((depth, 11)),
        ],
        compiler_params=pltpu.CompilerParams(
            collective_id=1, has_side_effects=True, vmem_limit_bytes=56 * 2**20
        ),
        name="scatter_sum",
    )(back_up, back_gate, w_up, w_gate)


def hidden_kernel(
    tok, cot, w_gate, w_up, w_down, scale, back_up, back_gate, back_t, hidden_t, gate, up, back
):
    step = pl.program_id(0)

    @pl.when(step == 0)
    def _():
        gate[...] = jnp.zeros_like(gate)
        up[...] = jnp.zeros_like(up)
        back[...] = jnp.zeros_like(back)

    gate[...] += dot(tok[...], w_gate[...], ((1,), (0,)))
    up[...] += dot(tok[...], w_up[...], ((1,), (0,)))
    back[...] += dot(cot[...], w_down[...], ((1,), (1,)))

    @pl.when(step == pl.num_programs(0) - 1)
    def _():
        size, units = 128, gate.shape[1]

        def body(i, carry):
            rows = pl.ds(pl.multiple_of(i * size, size), size)
            pre_gate, pre_up, factor = gate[rows, :], up[rows, :], scale[rows, :]
            sigma = jax.nn.sigmoid(pre_gate)
            activated = pre_gate * sigma
            back_hidden = factor * back[rows, :]
            hidden = (factor * activated * pre_up).astype(jnp.bfloat16)
            down_up = (back_hidden * activated).astype(jnp.bfloat16)
            down_gate = (
                back_hidden * pre_up * sigma * (1.0 + pre_gate * (1.0 - sigma))
            ).astype(jnp.bfloat16)
            back_up[rows, :] = down_up
            back_gate[rows, :] = down_gate
            hidden_t[:, rows] = hidden.T
            back_t[:units, rows] = down_gate.T
            back_t[units:, rows] = down_up.T
            return carry

        lax.fori_loop(0, gate.shape[0] // size, body, 0)


def hidden_grads(tok, cot, w_gate, w_up, w_down, scale):
    rows, width = tok.shape
    units = w_gate.shape[1]
    tile = 512
    kind = tok.dtype
    across = pl.BlockSpec((rows, tile), lambda i: (0, i))
    along = pl.BlockSpec((tile, units), lambda i: (i, 0))

    def fixed(shape):
        return pl.BlockSpec(shape, lambda i: (0, 0))

    shapes = [(rows, units), (rows, units), (2 * units, rows), (units, rows)]
    return pl.pallas_call(
        hidden_kernel,
        grid=(width // tile,),
        out_shape=[jax.ShapeDtypeStruct(s, kind) for s in shapes],
        in_specs=[
            across, across, along, along, pl.BlockSpec((units, tile), lambda i: (0, i)),
            fixed((rows, 1)),
        ],
        out_specs=[fixed(s) for s in shapes],
        scratch_shapes=[pltpu.VMEM((rows, units), jnp.float32)] * 3,
        compiler_params=pltpu.CompilerParams(vmem_limit_bytes=60 * 2**20),
        name="hidden_grads",
    )(tok, cot, w_gate, w_up, w_down, scale)


def weight_kernel(tok, cot, back_t, hidden_t, grad_gate, grad_up, grad_down):
    units = hidden_t.shape[0]
    both = dot(back_t[...], tok[...], ((1,), (0,))).astype(grad_gate.dtype)
    grad_gate[...] = both[:units].T
    grad_up[...] = both[units:].T
    grad_down[...] = dot(hidden_t[...], cot[...], ((1,), (0,))).astype(grad_down.dtype)


def weight_grads(tok, cot, back_t, hidden_t):
    rows, width = tok.shape
    units = hidden_t.shape[0]
    tile = 512
    kind = tok.dtype
    across = pl.BlockSpec((rows, tile), lambda i: (0, i))
    along = pl.BlockSpec((tile, units), lambda i: (i, 0))
    return pl.pallas_call(
        weight_kernel,
        grid=(width // tile,),
        out_shape=[
            jax.ShapeDtypeStruct((width, units), kind),
            jax.ShapeDtypeStruct((width, units), kind),
            jax.ShapeDtypeStruct((units, width), kind),
        ],
        in_specs=[
            across, across,
            pl.BlockSpec((2 * units, rows), lambda i: (0, 0)),
            pl.BlockSpec((units, rows), lambda i: (0, 0)),
        ],
        out_specs=[along, along, pl.BlockSpec((units, tile), lambda i: (0, i))],
        compiler_params=pltpu.CompilerParams(vmem_limit_bytes=40 * 2**20),
        name="weight_grads",
    )(tok, cot, back_t, hidden_t)


def per_device_dense(tokens, routes, route_gates, cotangent, weight_gate, weight_up, weight_down):
    me = lax.axis_index("expert")
    w_gate, w_up, w_down = weight_gate[0], weight_up[0], weight_down[0]

    owned = (routes[:, :, None] == jnp.arange(128, dtype=routes.dtype)).astype(jnp.float32)
    weight_of = jnp.sum(owned * route_gates.astype(jnp.float32)[:, :, None], axis=1)
    tok, cot, weight_all = gather_all([tokens, cotangent, weight_of.astype(jnp.bfloat16)])
    scale = lax.dynamic_slice_in_dim(weight_all, me, 1, 1).astype(jnp.float32)
    back_up, back_gate, back_t, hidden_t = hidden_grads(tok, cot, w_gate, w_up, w_down, scale)
    grad_tokens = scatter_sum(back_up, back_gate, w_up, w_gate)
    grad_gate, grad_up, grad_down = weight_grads(tok, cot, back_t, hidden_t)
    return (grad_tokens, grad_gate[None], grad_up[None], grad_down[None])


def solution(mesh):
    placed = (
        P("expert", None),
        P("expert", None),
        P("expert", None),
        P("expert", None),
        P("expert", None, "dp"),
        P("expert", None, "dp"),
        P("expert", "dp", None),
    )
    return jax.shard_map(
        per_device_dense if mesh.shape["expert"] <= 8 else per_device_slots,
        mesh=mesh,
        in_specs=placed,
        out_specs=(
            P("expert", "dp"),
            P("expert", None, "dp"),
            P("expert", None, "dp"),
            P("expert", "dp", None),
        ),
        check_vma=False,
    )
```
